256 devices in a mesh: grp: 4 (over z_hi), gx: 32 (over x, y, core), gy: 2 (over z_lo).
Axes of the slice: x: 4, y: 4, z: 8 (z_hi: 4, z_lo: 2; z = z_hi * 2 + z_lo), core: 2. Of those that a mesh axis runs over, the one named last changes fastest.
Arguments:
- state: float32 [8, 4, 125, 32, 256], P(('grp', 'gy'), None, None, 'gx'), may hold values from -6 to 6
- damping: float32 [32, 256], P('gx'), may hold values from 0.5 to 20
- absorb_mask: int32 [32, 256], P('gx'), may hold values 0 or 1
- lift_gain: float32 [64], replicated, may hold values from -3 to 3
- proj_weight: float32 [64], replicated, may hold values from -0.75 to 0.75
- spectral: float32 [4096, 64, 64], P('gx'), may hold values from -3 to 3
- moment_one: bfloat16 [4096, 64, 64], P('gx'), may hold values from -5 to 5
- moment_two: bfloat16 [4096, 64, 64], P('gx'), may hold values from 0.0099487305 to 1
Outputs:
- new_state: float32 [8, 4, 125, 32, 256], P(('grp', 'gy'), None, None, 'gx')
- new_spectral: float32 [4096, 64, 64], P('gx')
- new_moment_one: bfloat16 [4096, 64, 64], P('gx')
- new_moment_two: bfloat16 [4096, 64, 64], P('gx')
The draws below stay inside these ranges and needn't reach their ends.
All inputs are finite; a program needn't handle non-finite values. No bound on the sum of `absorb_mask` on one device may be relied on, other than what follows from the above.
Results may differ from the reference program's by a relative error of at most 0.0004.
Values may be sent and summed in bfloat16 or wider, within the bound.
A program may use at most 64 MiB of HBM per device.

```python
import math
import jax
import jax.numpy as jnp
import numpy as np
from jax import lax

CH = 64
KM = 16
TY = 64
TZ = 64
TX = 128
MODES = 4096
NXE = 32
EY = 16
EZ = 16
ELEMS = 256
SHOTS = 8
TILES = 8


def with_ends(drawn, stream_key, low, high):
    longest = drawn.shape.index(max(drawn.shape))
    spots = []
    for shift in (0, 1):
        where = [jax.random.randint(jax.random.fold_in(stream_key, axis), (), 0, length) for axis, length in enumerate(drawn.shape)]
        where[longest] = (where[longest] + shift) % drawn.shape[longest]
        spots.append(tuple(where))
    return drawn.at[spots[0]].set(low).at[spots[1]].set(high)


def steps_of(stream_key, shape, cuts, low, high):
    gain = 1.0
    for dim, shards_of in cuts:
        draws = jax.random.uniform(jax.random.fold_in(jax.random.fold_in(stream_key, 6), dim), (shards_of,), jnp.float32, low / len(cuts), high / len(cuts))
        gain = gain * jnp.repeat(jnp.exp(draws), shape[dim] // shards_of).reshape((-1,) + (1,) * (len(shape) - 1 - dim))
    return gain


def bell_draw(rng, dims, deviation, reach, pieces=(), held_as=jnp.bfloat16):
    loudness = steps_of(rng, dims, pieces, -0.22, 0.18) if pieces else 1.0
    values = jax.random.normal(rng, dims, jnp.float32) * deviation * loudness
    return jnp.minimum(jnp.maximum(values, -reach), reach).astype(held_as)


def setup_inputs(seed: int = 0) -> dict:
    splits = jax.random.split(jax.random.key(seed), 9)
    return {
        "state": bell_draw(splits[0], (SHOTS, 4, 125, NXE, ELEMS), 1.0, 6.0, ((0, 8), (3, 32)), jnp.float32),
        "damping": jnp.clip(jnp.exp(math.log(20.0) - 3.6888795 * jax.random.uniform(splits[1], (NXE, ELEMS), jnp.float32) ** steps_of(splits[1], (NXE, ELEMS), ((0, 32),), -0.2, 0.2)), 0.5, 20.0),
        "absorb_mask": with_ends((jax.random.randint(splits[2], (NXE, ELEMS), 0, 3) < 1).astype(jnp.int32), jax.random.fold_in(splits[2], 1), 0, 1),
        "lift_gain": bell_draw(splits[3], (CH,), 1.0, 3.0, (), jnp.float32),
        "proj_weight": bell_draw(splits[4], (CH,), CH ** -0.5, 0.75, (), jnp.float32),
        "spectral": bell_draw(splits[5], (MODES, CH, CH), 0.5, 3.0, ((0, 32),), jnp.float32),
        "moment_one": bell_draw(splits[6], (MODES, CH, CH), 1.0, 5.0, ((0, 32),)),
        "moment_two": jnp.clip(jnp.exp(math.log(1.0) - 4.61031033 * jax.random.uniform(splits[7], (MODES, CH, CH), jnp.float32) ** steps_of(splits[7], (MODES, CH, CH), ((0, 32),), -0.2, 0.2)), 0.0099487305, 1.0).astype(jnp.bfloat16),
    }


HIGHEST = lax.Precision.HIGHEST
TIME_STEP = 0.02
FACE_GAIN = 10.0
LOSS_SCALE = 1.0 / 2048.0
LEARN_RATE = 0.001
BETA_ONE = 0.9
BETA_TWO = 0.999
BIAS_ONE = 1.0 - BETA_ONE ** 10
BIAS_TWO = 1.0 - BETA_TWO ** 10
EPSILON = 1e-08
HALF_ROOT = 1.0 / math.sqrt(2.0)
GAUSS_NORM = 1.0 / math.sqrt(2.0 * math.pi)

def lagrange(gll_nodes, column, target_point):
    result_value = 1.0
    for other_node in range(len(gll_nodes)):
        if other_node != column:
            result_value = result_value * (target_point - gll_nodes[other_node]) / (gll_nodes[column] - gll_nodes[other_node])
    return result_value

def lagrange_slope(gll_nodes, column, target_point):
    slope_total = 0.0
    for skipped in range(len(gll_nodes)):
        if skipped != column:
            factor = 1.0 / (gll_nodes[column] - gll_nodes[skipped])
            for other_node in range(len(gll_nodes)):
                if other_node != column and other_node != skipped:
                    factor = factor * (target_point - gll_nodes[other_node]) / (gll_nodes[column] - gll_nodes[other_node])
            slope_total = slope_total + factor
    return slope_total

def gll_tables():
    gll_nodes = [-1.0, -math.sqrt(3.0 / 7.0), 0.0, math.sqrt(3.0 / 7.0), 1.0]
    slopes = np.zeros((5, 5))
    interp = np.zeros((4, 5))
    for node_row in range(5):
        for column in range(5):
            slopes[node_row, column] = lagrange_slope(gll_nodes, column, gll_nodes[node_row])
    for sample in range(4):
        for column in range(5):
            interp[sample, column] = lagrange(gll_nodes, column, -1.0 + (2.0 * sample + 1.0) / 4.0)
    return (jnp.asarray(slopes, dtype=jnp.float32), jnp.asarray(interp, dtype=jnp.float32))

def fourier_table(length, kept):
    angles = np.arange(length) * (2.0 * math.pi / length)
    table_rows = []
    for freq_index in range(kept // 2 + 1):
        factor = math.sqrt(1.0 / length) if freq_index == 0 else math.sqrt(2.0 / length)
        table_rows.append(factor * np.cos(freq_index * angles))
    for freq_index in range(1, kept // 2):
        table_rows.append(math.sqrt(2.0 / length) * np.sin(freq_index * angles))
    return np.stack(table_rows)

def joint_table(length_y, length_z, kept):
    joined = np.kron(fourier_table(length_y, kept), fourier_table(length_z, kept))
    return jnp.asarray(joined, dtype=jnp.float32).astype(jnp.bfloat16)

def apply_along(matrix, field_values, node_axis):
    applied = jnp.tensordot(matrix, field_values, axes=((1,), (node_axis,)), precision=HIGHEST)
    return jnp.moveaxis(applied, 0, node_axis)

def shift_elements(pack, elem_step, z_count, along_z):
    total_elems = pack.shape[-1]
    padding = jnp.zeros(pack.shape[:-1] + (abs(elem_step),), pack.dtype)
    if elem_step > 0:
        shifted = jnp.concatenate([padding, pack[..., :total_elems - elem_step]], axis=-1)
    else:
        shifted = jnp.concatenate([pack[..., -elem_step:], padding], axis=-1)
    if along_z:
        position = lax.broadcasted_iota(jnp.int32, (total_elems,), 0) % z_count
        edge_index = 0 if elem_step > 0 else z_count - 1
        shifted = jnp.where(position == edge_index, 0.0, shifted)
    return shifted

def place_faces(low_face, high_face, node_axis):
    empty_face = jnp.zeros_like(low_face)
    return jnp.stack([low_face, empty_face, empty_face, empty_face, high_face], axis=node_axis)

def rates_of(fields, sink_rate, x_neighbours, z_count, slopes):
    pressure = fields[0]
    pressure_rate = jnp.zeros_like(pressure)
    velocity_rates = []
    for direction in range(3):
        velocity = fields[1 + direction]
        pressure_rate = pressure_rate - 2.0 * apply_along(slopes, velocity, direction)
        change = -2.0 * apply_along(slopes, pressure, direction)
        low_pack = jnp.stack([jnp.take(pressure, 0, axis=direction), jnp.take(velocity, 0, axis=direction)])
        high_pack = jnp.stack([jnp.take(pressure, 4, axis=direction), jnp.take(velocity, 4, axis=direction)])
        if direction == 0:
            from_low, from_high = x_neighbours(low_pack, high_pack)
        else:
            elem_step = z_count if direction == 1 else 1
            from_low = shift_elements(high_pack, elem_step, z_count, direction == 2)
            from_high = shift_elements(low_pack, -elem_step, z_count, direction == 2)
        jump_low = low_pack - from_low
        jump_high = high_pack - from_high
        low_rate = -FACE_GAIN * (jump_low[1] + jump_low[0])
        high_rate = FACE_GAIN * (jump_high[1] - jump_high[0])
        pressure_rate = pressure_rate + place_faces(low_rate, high_rate, direction)
        change = change + place_faces(low_rate, -high_rate, direction)
        velocity_rates.append(change)
    rates = jnp.stack([pressure_rate] + velocity_rates)
    return rates - sink_rate * fields

def advance(fields, sink_rate, x_neighbours, z_count, slopes):
    first_rate = rates_of(fields, sink_rate, x_neighbours, z_count, slopes)
    mid_section = fields + TIME_STEP * first_rate
    second_rate = rates_of(mid_section, sink_rate, x_neighbours, z_count, slopes)
    return 0.5 * (fields + mid_section + TIME_STEP * second_rate)

def regrid(pressure, interp):
    result_grid = apply_along(interp, pressure, 0)
    result_grid = apply_along(interp, result_grid, 1)
    return apply_along(interp, result_grid, 2)

def lift_field(inputs, lift_gain):
    scaled = lift_gain[None, :, None, None] * inputs[:, None].astype(jnp.float32)
    return jax.nn.gelu(scaled, approximate=False).astype(jnp.bfloat16)

def to_basis(field_values, table_x, table_yz, kept):
    along_yz = jnp.einsum('tcxp,qp->tcxq', field_values.astype(jnp.float32), table_yz.astype(jnp.float32), precision=HIGHEST)
    basis_coeffs = jnp.einsum('tcxq,ax->aqtc', along_yz, table_x.astype(jnp.float32), precision=HIGHEST)
    return basis_coeffs.reshape(kept * kept * kept, field_values.shape[0], field_values.shape[1])

def from_basis(mixed_modes, table_x, table_yz, kept):
    shaped = mixed_modes.reshape(kept, kept * kept, mixed_modes.shape[1], mixed_modes.shape[2])
    along_x = jnp.einsum('aqto,ax->toxq', shaped.astype(jnp.float32), table_x.astype(jnp.float32), precision=HIGHEST)
    return jnp.einsum('toxq,qp->toxp', along_x, table_yz.astype(jnp.float32), precision=HIGHEST)

def backward(pre_act, targets, proj_weight):
    active = jax.nn.gelu(pre_act, approximate=False)
    predicted = jnp.einsum('toxp,o->txp', active, proj_weight, precision=HIGHEST)
    misfit = predicted - targets.astype(jnp.float32)
    gelu_slope = 0.5 * (1.0 + lax.erf(pre_act * HALF_ROOT)) + pre_act * jnp.exp(-0.5 * pre_act * pre_act) * GAUSS_NORM
    scaled = 2.0 * LOSS_SCALE * misfit[:, None] * proj_weight[None, :, None, None] * gelu_slope
    return scaled.astype(jnp.bfloat16)

def adam_update(spectral, moment_one, moment_two, gradient):
    first_moment = BETA_ONE * moment_one.astype(jnp.float32) + (1.0 - BETA_ONE) * gradient
    second_moment = BETA_TWO * moment_two.astype(jnp.float32) + (1.0 - BETA_TWO) * gradient * gradient
    denominator = jnp.sqrt(second_moment / BIAS_TWO) + EPSILON
    new_spectral = spectral - LEARN_RATE * (first_moment / BIAS_ONE) / denominator
    return (new_spectral, first_moment.astype(jnp.bfloat16), second_moment.astype(jnp.bfloat16))

def shift_slabs(pack, slab_step):
    slab_total = pack.shape[-2]
    padding = jnp.zeros_like(pack[..., :1, :])
    if slab_step > 0:
        return jnp.concatenate([padding, pack[..., :slab_total - 1, :]], axis=-2)
    return jnp.concatenate([pack[..., 1:, :], padding], axis=-2)

def slab_neighbours(low_pack, high_pack):
    return (shift_slabs(high_pack, 1), shift_slabs(low_pack, -1))

def reference(state, damping, absorb_mask, lift_gain, proj_weight, spectral, moment_one, moment_two):
    slopes, interp = gll_tables()
    sink_rate = absorb_mask.astype(jnp.float32) * damping

    def one_shot(shot_state):
        fields = shot_state.reshape(4, 5, 5, 5, NXE, ELEMS)
        new_fields = advance(fields, sink_rate, slab_neighbours, EZ, slopes)
        snap_pair = jnp.stack([regrid(fields[0], interp), regrid(new_fields[0], interp)]).astype(jnp.bfloat16)
        return (new_fields.reshape(4, 125, NXE, ELEMS), snap_pair)
    new_state, snap_pairs = lax.map(one_shot, state)
    snap_pairs = snap_pairs.reshape(SHOTS, 2, 4, 4, 4, NXE, EY, EZ)
    tile_data = jnp.transpose(snap_pairs, (0, 1, 5, 2, 6, 3, 7, 4)).reshape(TILES, 2, TX, TY * TZ)
    table_x = jnp.asarray(fourier_table(TX, KM), dtype=jnp.float32).astype(jnp.bfloat16)
    table_yz = joint_table(TY, TZ, KM)

    def per_tile(grad_total, one_tile):
        inputs = one_tile[0][None]
        targets = one_tile[1][None]
        lifted = lift_field(inputs, lift_gain)
        coeffs = to_basis(lifted, table_x, table_yz, KM)
        mixed_modes = jnp.einsum('mtc,mco->mto', coeffs, spectral, precision=HIGHEST).astype(jnp.bfloat16)
        pre_act = from_basis(mixed_modes, table_x, table_yz, KM)
        grad_pre = backward(pre_act, targets, proj_weight)
        grad_coeffs = to_basis(grad_pre, table_x, table_yz, KM)
        contribution = jnp.einsum('mtc,mto->mco', coeffs, grad_coeffs, precision=HIGHEST)
        return (grad_total + contribution, None)
    gradient, unused = lax.scan(per_tile, jnp.zeros((MODES, CH, CH), jnp.float32), tile_data)
    new_spectral, new_moment_one, new_moment_two = adam_update(spectral, moment_one, moment_two, gradient)
    return (new_state, new_spectral, new_moment_one, new_moment_two)
```

```python
import math

import jax
import jax.numpy as jnp
import numpy as np
from jax import lax
from jax.experimental import pallas as pl
from jax.experimental.pallas import tpu as pltpu
from jax.sharding import PartitionSpec as P

MESH = pl.DeviceIdType.MESH
HIGHEST = lax.Precision.HIGHEST
KM = 16
CHIPS = 16
ZPEERS = 8
TIME_STEP = 0.02
FACE_GAIN = 10.0
LOSS_SCALE = 1.0 / 2048.0
LEARN_RATE = 0.001
BETA_ONE = 0.9
BETA_TWO = 0.999
BIAS_ONE = 1.0 - BETA_ONE**10
BIAS_TWO = 1.0 - BETA_TWO**10
EPSILON = 1e-08
HALF_ROOT = 1.0 / math.sqrt(2.0)
GAUSS_NORM = 1.0 / math.sqrt(2.0 * math.pi)
LOG2E = 1.4426950408889634


def lagrange(nodes, column, point):
    value = 1.0
    for other in range(len(nodes)):
        if other != column:
            value = value * (point - nodes[other]) / (nodes[column] - nodes[other])
    return value


def lagrange_slope(nodes, column, point):
    total = 0.0
    for skipped in range(len(nodes)):
        if skipped != column:
            factor = 1.0 / (nodes[column] - nodes[skipped])
            for other in range(len(nodes)):
                if other != column and other != skipped:
                    factor = factor * (point - nodes[other]) / (nodes[column] - nodes[other])
            total = total + factor
    return total


def gll_tables():
    nodes = [-1.0, -math.sqrt(3.0 / 7.0), 0.0, math.sqrt(3.0 / 7.0), 1.0]
    slopes = np.array([[lagrange_slope(nodes, c, nodes[r]) for c in range(5)] for r in range(5)])
    interp = np.array(
        [[lagrange(nodes, c, -1.0 + (2.0 * m + 1.0) / 4.0) for c in range(5)] for m in range(4)]
    )
    return slopes.astype(np.float32), interp.astype(np.float32)


def fourier_table(length, kept):
    angles = np.arange(length) * (2.0 * math.pi / length)
    rows = []
    for freq in range(kept // 2 + 1):
        factor = math.sqrt(1.0 / length) if freq == 0 else math.sqrt(2.0 / length)
        rows.append(factor * np.cos(freq * angles))
    for freq in range(1, kept // 2):
        rows.append(math.sqrt(2.0 / length) * np.sin(freq * angles))
    return np.stack(rows)


def node_of(index, axis, value):
    out = list(index)
    out[axis] = value
    return 25 * out[0] + 5 * out[1] + out[2]


def solver_tables(slopes):
    own = np.zeros((512, 512))
    near = np.zeros((512, 192))
    pick = np.zeros((192, 512))
    for i1 in range(5):
        for i2 in range(5):
            for i3 in range(5):
                index = (i1, i2, i3)
                node = 25 * i1 + 5 * i2 + i3
                for d in range(3):
                    u = 125 * (1 + d)
                    for k in range(5):
                        other = node_of(index, d, k)
                        own[node, u + other] += -2.0 * slopes[index[d], k]
                        own[u + node, other] += -2.0 * slopes[index[d], k]
                    rest = [index[e] for e in range(3) if e != d]
                    face = 5 * rest[0] + rest[1]
                    low, high = 64 * d + face, 64 * d + 32 + face
                    if index[d] == 0:
                        own[node, u + node] -= FACE_GAIN
                        own[node, node] -= FACE_GAIN
                        own[u + node, u + node] -= FACE_GAIN
                        own[u + node, node] -= FACE_GAIN
                        near[node, low] = FACE_GAIN
                        near[u + node, low] = FACE_GAIN
                        pick[high, node] = 1.0
                        pick[high, u + node] = -1.0
                    if index[d] == 4:
                        own[node, u + node] += FACE_GAIN
                        own[node, node] -= FACE_GAIN
                        own[u + node, node] += FACE_GAIN
                        own[u + node, u + node] -= FACE_GAIN
                        near[node, high] = FACE_GAIN
                        near[u + node, high] = -FACE_GAIN
                        pick[low, node] = 1.0
                        pick[low, u + node] = 1.0
    return tuple(t.astype(np.float32) for t in (own, near, pick))


def tables():
    slopes, interp = gll_tables()
    own, near, pick = solver_tables(slopes.astype(np.float64))
    interp = interp.astype(np.float64)
    regrid = np.zeros((64, 128), np.float32)
    regrid[:, :125] = np.kron(np.kron(interp, interp), interp).astype(np.float32)
    joint = np.kron(fourier_table(64, KM), fourier_table(64, KM)).astype(np.float32)
    joint = joint.reshape(256, 16, 4, 16, 4).transpose(2, 4, 0, 1, 3).reshape(16, 256, 256)
    inverse = jnp.asarray(joint).astype(jnp.bfloat16)
    forward = jnp.asarray(joint.transpose(0, 2, 1)).astype(jnp.bfloat16)
    along_x = jnp.asarray(fourier_table(128, KM), dtype=jnp.float32).astype(jnp.bfloat16)
    along_x = along_x.astype(jnp.float32).reshape(-1)
    return own, near, pick, regrid, forward, inverse, along_x


def normal_parts(x):
    bell = jnp.exp2(x * x * (-0.5 * LOG2E))
    den = 1.0 + (0.3275911 * HALF_ROOT) * jnp.abs(x)
    t = pl.reciprocal(den, approx=True)
    t = t * (2.0 - den * t)
    poly = 0.5 * 1.061405429 * t - 0.5 * 1.453152027
    poly = poly * t + 0.5 * 1.421413741
    poly = poly * t - 0.5 * 0.284496736
    poly = poly * t + 0.5 * 0.254829592
    tail = poly * t * bell
    return jnp.where(x >= 0.0, 1.0 - tail, tail), bell


def dot_f32(a, b):
    return jnp.dot(a, b, precision=HIGHEST, preferred_element_type=jnp.float32)


def dot_bf16(a, b):
    return jnp.dot(a, b, preferred_element_type=jnp.float32)


def column(row):
    eye = lax.broadcasted_iota(jnp.int32, (64, 64), 0) == lax.broadcasted_iota(
        jnp.int32, (64, 64), 1
    )
    col = jnp.sum(jnp.where(eye, row, 0.0), axis=1, keepdims=True)
    return jnp.broadcast_to(col, (64, 256))


def step_kernel(
    state, damping, mask, gain, weight, pick, regrid, table_x, own_h, near_h, spec_h, fwd_h, inv_h,
    new_state, coef_all, grad_all,
    own, near, spec, fwd, inv,
    q, sec, faces, halo, edge, sink, a, b, gcol, wcol, g, pre, slope,
    fwd_sum, sib_sum, parts, inbox, total, mixed, ax, ax_hi, ax_lo,
    load_sem, halo_s, halo_r, sib_s, sib_r, part_s, part_r, mix_s, mix_r, hop_s, hop_r, z_s, z_r,
):
    grp, gx, gy = lax.axis_index("grp"), lax.axis_index("gx"), lax.axis_index("gy")
    chip, core = lax.div(gx, 2), lax.rem(gx, 2)
    cx, cy = lax.div(chip, 4), lax.rem(chip, 4)
    zme = grp * 2 + gy
    sibling = gx + 1 - 2 * core

    def chip_at(k, sign):
        dx, dy = lax.div(k, 4), lax.rem(k, 4)
        return lax.rem(cx + sign * dx + 4, 4) * 4 + lax.rem(cy + sign * dy + 4, 4)

    def z_at(k):
        zt = lax.rem(zme + k, ZPEERS)
        return {"grp": lax.div(zt, 2), "gy": lax.rem(zt, 2)}

    def each(lo, hi, f, unroll=1):
        def step(k, carry):
            f(k)
            return carry
        lax.fori_loop(lo, hi, step, 0, unroll=unroll)

    loads = [
        pltpu.make_async_copy(src, dst, load_sem.at[i])
        for i, (src, dst) in enumerate(
            ((fwd_h, fwd), (own_h, own), (near_h, near), (spec_h, spec), (inv_h, inv))
        )
    ]
    for c in loads:
        c.start()

    barrier = pltpu.get_barrier_semaphore()

    def greet(target):
        pl.semaphore_signal(barrier, inc=1, device_id=target, device_id_type=MESH)

    each(1, CHIPS, lambda k: greet({"gx": 2 * chip_at(k, 1) + core}))
    greet({"gx": sibling})
    greet({"gx": lax.rem(gx + 2 * core + 31, 32)})
    each(1, ZPEERS, lambda k: greet(z_at(k)))

    q[0:500, 0:128] = state[pl.ds(0, 500, stride=2), :]
    q[0:500, 128:256] = state[pl.ds(1, 500, stride=2), :]
    q[500:512, :] = jnp.zeros((12, 256), jnp.float32)
    a[...] = dot_f32(regrid[...], q[0:128, :]).astype(jnp.bfloat16).astype(jnp.float32)
    faces[0] = dot_f32(pick[...], q[...])
    gcol[...] = column(gain[...])
    wcol[...] = column(weight[...])
    sink[...] = mask[...].astype(jnp.float32) * damping[...]
    fwd_sum[...] = jnp.zeros_like(fwd_sum)

    pl.semaphore_wait(barrier, CHIPS - 1 + 2 + ZPEERS - 1)

    def halo_copy(stage, side):
        to = lax.rem(gx + (1, 31)[side], 32)
        return pltpu.make_async_remote_copy(
            src_ref=faces.at[stage, pl.ds(32 * side, 32)],
            dst_ref=halo.at[stage, side],
            send_sem=halo_s.at[stage, side],
            recv_sem=halo_r.at[stage, side],
            device_id={"gx": to},
            device_id_type=MESH,
        )

    for side in range(2):
        halo_copy(0, side).start()

    loads[0].wait()

    def transform(phase, j, slot):
        both = dot_bf16(g[slot], fwd[j])
        fwd_sum[phase, 0] += both[:, 0:128]
        fwd_sum[phase, 1] += both[:, 128:256]

    def lift(j, slot):
        for m in range(4):
            row = a[pl.ds(m * 16 + j, 1), :]
            for r in range(2):
                rows = pl.ds(32 * r, 32)
                x = gcol[rows, :] * row
                cdf, unused = normal_parts(x)
                g[slot, pl.ds(64 * m + 32 * r, 32), :] = (x * cdf).astype(jnp.bfloat16)
        transform(0, j, slot)

    def lift_pair(i):
        lift(2 * i, 0)
        lift(2 * i + 1, 1)

    each(0, 8, lift_pair)

    def sib_copy(phase):
        return pltpu.make_async_remote_copy(
            src_ref=fwd_sum.at[phase, 1 - core],
            dst_ref=sib_sum.at[phase],
            send_sem=sib_s.at[phase],
            recv_sem=sib_r.at[phase],
            device_id={"gx": sibling},
            device_id_type=MESH,
        )

    def part_copy(phase, k):
        return pltpu.make_async_remote_copy(
            src_ref=parts.at[phase, k],
            dst_ref=inbox.at[phase, k],
            send_sem=part_s.at[phase, k],
            recv_sem=part_r.at[phase, k],
            device_id={"gx": 2 * chip_at(k, 1) + core},
            device_id_type=MESH,
        )

    def expand(phase, k):
        base = chip_at(k, 1) * 128 + 8 * chip
        acc = jnp.zeros((64, 128), jnp.float32)
        for m in range(4):
            rows = pl.ds(64 * m, 64)
            acc = acc + table_x[base + 4 * core + m] * fwd_sum[phase, core, rows, :]
            acc = acc + table_x[base + 4 - 4 * core + m] * sib_sum[phase, rows, :]
        return acc

    def scatter(phase):
        sib_copy(phase).start()
        sib_copy(phase).wait()

        def send(k):
            parts[phase, k] = expand(phase, k)
            part_copy(phase, k).start()

        each(1, CHIPS, send)
        total[phase] = expand(phase, 0)

    def gather_sum(phase):
        def add(k, acc):
            part_copy(phase, k).wait_recv()
            return acc + inbox[phase, k]

        return lax.fori_loop(1, CHIPS, add, total[phase])

    def z_copy(phase, k):
        ref = (coef_all, grad_all)[phase]
        return pltpu.make_async_remote_copy(
            src_ref=ref.at[zme],
            dst_ref=ref.at[zme],
            send_sem=z_s.at[phase, k],
            recv_sem=z_r.at[phase, k],
            device_id=z_at(k),
            device_id_type=MESH,
        )

    lanes = lax.broadcasted_iota(jnp.int32, (32, 256), 1)
    ez = lax.rem(lanes, 16)

    def rates(stage, fields):
        for side in range(2):
            halo_copy(stage, side).wait_recv()
        ends = (gx == 0, gx == 31)
        for side in range(2):
            edge[pl.ds(32 * side, 32), :] = jnp.where(ends[side], 0.0, halo[stage, side])
        low, high = faces[stage, 64:96, :], faces[stage, 96:128, :]
        edge[64:96, :] = jnp.where(lanes < 16, 0.0, pltpu.roll(low, 16, 1))
        edge[96:128, :] = jnp.where(lanes >= 240, 0.0, pltpu.roll(high, 240, 1))
        low, high = faces[stage, 128:160, :], faces[stage, 160:192, :]
        edge[128:160, :] = jnp.where(ez == 0, 0.0, pltpu.roll(low, 1, 1))
        edge[160:192, :] = jnp.where(ez == 15, 0.0, pltpu.roll(high, 255, 1))
        rate = dot_f32(own[...], fields[...]) + dot_f32(near[...], edge[...])
        return rate - sink[...] * fields[...]

    scatter(0)

    loads[1].wait()
    loads[2].wait()
    sec[...] = q[...] + TIME_STEP * rates(0, q)
    faces[1] = dot_f32(pick[...], sec[...])
    for side in range(2):
        halo_copy(1, side).start()

    coef_all[pl.ds(zme, 1)] = gather_sum(0)[None]
    each(1, ZPEERS, lambda k: z_copy(0, k).start())

    loads[3].wait()

    def mix(i, acc):
        for u in range(8):
            c = i * 8 + u
            row = coef_all[pl.ds(zme, 1), pl.ds(c, 1), :].reshape(1, 128)
            acc = acc + spec[c] * row
        return acc

    mixed[0, 0] = lax.fori_loop(0, 8, mix, jnp.zeros((64, 128), jnp.float32)).astype(jnp.bfloat16)

    def mix_copy(k):
        return pltpu.make_async_remote_copy(
            src_ref=mixed.at[0, 0],
            dst_ref=mixed.at[0, k],
            send_sem=mix_s.at[k],
            recv_sem=mix_r.at[k],
            device_id={"gx": 2 * chip_at(k, 1) + core},
            device_id_type=MESH,
        )

    def hop_copy(k):
        return pltpu.make_async_remote_copy(
            src_ref=mixed.at[0, k],
            dst_ref=mixed.at[1, k],
            send_sem=hop_s.at[k],
            recv_sem=hop_r.at[k],
            device_id={"gx": sibling},
            device_id_type=MESH,
        )

    each(1, CHIPS, lambda k: mix_copy(k).start())
    hop_copy(0).start()

    done = 0.5 * (q[...] + sec[...] + TIME_STEP * rates(1, sec))
    new_state[pl.ds(0, 500, stride=2), :] = done[0:500, 0:128]
    new_state[pl.ds(1, 500, stride=2), :] = done[0:500, 128:256]
    b[...] = dot_f32(regrid[...], done[0:128, :]).astype(jnp.bfloat16).astype(jnp.float32)

    def add_modes(half, k, acc):
        base = chip_at(k, -1) * 128 + 4 * gx
        value = mixed[half, k].astype(jnp.float32)
        return tuple(acc[m] + table_x[base + m] * value for m in range(4))

    def own_half(k, acc):
        mix_copy(k).wait_recv()
        hop_copy(k).start()
        return add_modes(0, k, acc)

    def other_half(k, acc):
        hop_copy(k).wait_recv()
        return add_modes(1, k, acc)

    zeros = tuple(jnp.zeros((64, 128), jnp.float32) for unused in range(4))
    sums = lax.fori_loop(1, CHIPS, own_half, add_modes(0, 0, zeros))
    for m in range(4):
        ax[pl.ds(core, 1), pl.ds(64 * m, 64), :] = sums[m][None]
    sums = lax.fori_loop(0, CHIPS, other_half, zeros)
    for m in range(4):
        ax[pl.ds(1 - core, 1), pl.ds(64 * m, 64), :] = sums[m][None]
    for half in range(2):
        value = ax[half]
        high = value.astype(jnp.bfloat16)
        ax_hi[:, 128 * half : 128 * half + 128] = high
        ax_lo[:, 128 * half : 128 * half + 128] = (value - high.astype(jnp.float32)).astype(
            jnp.bfloat16
        )

    loads[4].wait()

    def back(j, slot):
        pre[slot] = dot_bf16(ax_hi[...], inv[j]) + dot_bf16(ax_lo[...], inv[j])
        for m in range(4):
            acc = jnp.zeros((8, 256), jnp.float32)
            for r in range(2):
                rows = pl.ds(64 * m + 32 * r, 32)
                x = pre[slot, rows, :]
                cdf, bell = normal_parts(x)
                slope[slot, rows, :] = cdf + x * bell * GAUSS_NORM
                act = x * cdf * wcol[pl.ds(32 * r, 32), :]
                acc = acc + jnp.sum(act.reshape(4, 8, 256), axis=0)
            misfit = jnp.sum(acc, axis=0, keepdims=True) - b[pl.ds(m * 16 + j, 1), :]
            misfit = (2.0 * LOSS_SCALE) * misfit
            for r in range(2):
                rows = pl.ds(64 * m + 32 * r, 32)
                value = misfit * wcol[pl.ds(32 * r, 32), :] * slope[slot, rows, :]
                g[slot, rows, :] = value.astype(jnp.bfloat16)
        transform(1, j, slot)

    def back_pair(i):
        back(2 * i, 0)
        back(2 * i + 1, 1)

    each(0, 8, back_pair)

    scatter(1)
    grad_all[pl.ds(zme, 1)] = gather_sum(1)[None]
    each(1, ZPEERS, lambda k: z_copy(1, k).start())

    def drain_chip(k):
        part_copy(0, k).wait_send()
        part_copy(1, k).wait_send()
        mix_copy(k).wait_send()

    each(1, CHIPS, drain_chip)
    each(0, CHIPS, lambda k: hop_copy(k).wait_send())
    for stage in range(2):
        for side in range(2):
            halo_copy(stage, side).wait_send()

    def drain_z(k):
        z_copy(0, k).wait()
        z_copy(1, k).wait()

    each(1, ZPEERS, drain_z)


def adam_kernel(coef, grad, spec, one, two, new_spec, new_one, new_two):
    block = spec.shape[0]
    first = pl.program_id(0) * block
    for c in range(block):
        acc = coef[0, pl.ds(first + c, 1), :] * grad[0]
        for t in range(1, ZPEERS):
            acc = acc + coef[t, pl.ds(first + c, 1), :] * grad[t]
        m1 = BETA_ONE * one[c].astype(jnp.float32) + (1.0 - BETA_ONE) * acc
        m2 = BETA_TWO * two[c].astype(jnp.float32) + (1.0 - BETA_TWO) * acc * acc
        den = jnp.sqrt(m2 * (1.0 / BIAS_TWO)) + EPSILON
        new_spec[c] = spec[c] - (LEARN_RATE / BIAS_ONE) * m1 / den
        new_one[c] = m1.astype(jnp.bfloat16)
        new_two[c] = m2.astype(jnp.bfloat16)


def per_device(state, damping, mask, gain, weight, spectral, moment_one, moment_two):
    own, near, pick, regrid, forward, inverse, along_x = tables()
    f32, bf16 = jnp.float32, jnp.bfloat16
    vmem = pl.BlockSpec(memory_space=pltpu.VMEM)
    smem = pl.BlockSpec(memory_space=pltpu.SMEM)
    anywhere = pl.BlockSpec(memory_space=pl.ANY)
    spec_t = jnp.transpose(spectral, (1, 2, 0))
    dma = pltpu.SemaphoreType.DMA
    new_state, coef_all, grad_all = pl.pallas_call(
        step_kernel,
        out_shape=(
            jax.ShapeDtypeStruct((1000, 128), f32),
            jax.ShapeDtypeStruct((ZPEERS, 64, 128), f32),
            jax.ShapeDtypeStruct((ZPEERS, 64, 128), f32),
        ),
        in_specs=[vmem] * 7 + [smem] + [anywhere] * 5,
        out_specs=(vmem, vmem, vmem),
        scratch_shapes=[
            pltpu.VMEM((512, 512), f32),
            pltpu.VMEM((512, 192), f32),
            pltpu.VMEM((64, 64, 128), f32),
            pltpu.VMEM((16, 256, 256), bf16),
            pltpu.VMEM((16, 256, 256), bf16),
            pltpu.VMEM((512, 256), f32),
            pltpu.VMEM((512, 256), f32),
            pltpu.VMEM((2, 192, 256), f32),
            pltpu.VMEM((2, 2, 32, 256), f32),
            pltpu.VMEM((192, 256), f32),
            pltpu.VMEM((1, 256), f32),
            pltpu.VMEM((64, 256), f32),
            pltpu.VMEM((64, 256), f32),
            pltpu.VMEM((64, 256), f32),
            pltpu.VMEM((64, 256), f32),
            pltpu.VMEM((2, 256, 256), bf16),
            pltpu.VMEM((2, 256, 256), f32),
            pltpu.VMEM((2, 256, 256), f32),
            pltpu.VMEM((2, 2, 256, 128), f32),
            pltpu.VMEM((2, 256, 128), f32),
            pltpu.VMEM((2, CHIPS, 64, 128), f32),
            pltpu.VMEM((2, CHIPS, 64, 128), f32),
            pltpu.VMEM((2, 64, 128), f32),
            pltpu.VMEM((2, CHIPS, 64, 128), bf16),
            pltpu.VMEM((2, 256, 128), f32),
            pltpu.VMEM((256, 256), bf16),
            pltpu.VMEM((256, 256), bf16),
            dma((5,)),
            dma((2, 2)),
            dma((2, 2)),
            dma((2,)),
            dma((2,)),
            dma((2, CHIPS)),
            dma((2, CHIPS)),
            dma((CHIPS,)),
            dma((CHIPS,)),
            dma((CHIPS,)),
            dma((CHIPS,)),
            dma((2, ZPEERS)),
            dma((2, ZPEERS)),
        ],
        compiler_params=pltpu.CompilerParams(
            collective_id=0, has_side_effects=True, vmem_limit_bytes=40 * 1024 * 1024
        ),
        name="step",
    )(
        state.reshape(1000, 128), damping, mask, gain.reshape(1, 64), weight.reshape(1, 64),
        pick, regrid, along_x, own, near, spec_t, forward, inverse,
    )
    block = 8
    whole = pl.BlockSpec((ZPEERS, 64, 128), lambda i: (0, 0, 0))
    tile = pl.BlockSpec((block, 64, 128), lambda i: (i, 0, 0))
    new_spec, new_one, new_two = pl.pallas_call(
        adam_kernel,
        grid=(64 // block,),
        out_shape=(
            jax.ShapeDtypeStruct((64, 64, 128), f32),
            jax.ShapeDtypeStruct((64, 64, 128), bf16),
            jax.ShapeDtypeStruct((64, 64, 128), bf16),
        ),
        in_specs=[whole, whole, tile, tile, tile],
        out_specs=(tile, tile, tile),
        compiler_params=pltpu.CompilerParams(vmem_limit_bytes=16 * 1024 * 1024),
        name="update",
    )(
        coef_all, grad_all, spec_t,
        jnp.transpose(moment_one, (1, 2, 0)), jnp.transpose(moment_two, (1, 2, 0)),
    )
    back = (2, 0, 1)
    return (
        new_state.reshape(state.shape),
        jnp.transpose(new_spec, back),
        jnp.transpose(new_one, back),
        jnp.transpose(new_two, back),
    )


def solution(mesh):
    in_specs = (
        P(("grp", "gy"), None, None, "gx", None),
        P("gx", None),
        P("gx", None),
        P(),
        P(),
        P("gx", None, None),
        P("gx", None, None),
        P("gx", None, None),
    )
    out_specs = (
        P(("grp", "gy"), None, None, "gx", None),
        P("gx", None, None),
        P("gx", None, None),
        P("gx", None, None),
    )
    return jax.shard_map(
        per_device, mesh=mesh, in_specs=in_specs, out_specs=out_specs, check_vma=False
    )
```

```python
import math

import jax
import jax.numpy as jnp
import numpy as np
from jax import lax
from jax.experimental import pallas as pl
from jax.experimental.pallas import tpu as pltpu
from jax.sharding import PartitionSpec as P

MESH = pl.DeviceIdType.MESH
HIGHEST = lax.Precision.HIGHEST
KM = 16
CHIPS = 16
ZPEERS = 8
TIME_STEP = 0.02
FACE_GAIN = 10.0
LOSS_SCALE = 1.0 / 2048.0
LEARN_RATE = 0.001
BETA_ONE = 0.9
BETA_TWO = 0.999
BIAS_ONE = 1.0 - BETA_ONE**10
BIAS_TWO = 1.0 - BETA_TWO**10
EPSILON = 1e-08
HALF_ROOT = 1.0 / math.sqrt(2.0)
GAUSS_NORM = 1.0 / math.sqrt(2.0 * math.pi)
LOG2E = 1.4426950408889634


def lagrange(nodes, column, point):
    value = 1.0
    for other in range(len(nodes)):
        if other != column:
            value = value * (point - nodes[other]) / (nodes[column] - nodes[other])
    return value


def lagrange_slope(nodes, column, point):
    total = 0.0
    for skipped in range(len(nodes)):
        if skipped != column:
            factor = 1.0 / (nodes[column] - nodes[skipped])
            for other in range(len(nodes)):
                if other != column and other != skipped:
                    factor = factor * (point - nodes[other]) / (nodes[column] - nodes[other])
            total = total + factor
    return total


def gll_tables():
    nodes = [-1.0, -math.sqrt(3.0 / 7.0), 0.0, math.sqrt(3.0 / 7.0), 1.0]
    slopes = np.array([[lagrange_slope(nodes, c, nodes[r]) for c in range(5)] for r in range(5)])
    interp = np.array(
        [[lagrange(nodes, c, -1.0 + (2.0 * m + 1.0) / 4.0) for c in range(5)] for m in range(4)]
    )
    return slopes.astype(np.float32), interp.astype(np.float32)


def fourier_table(length, kept):
    angles = np.arange(length) * (2.0 * math.pi / length)
    rows = []
    for freq in range(kept // 2 + 1):
        factor = math.sqrt(1.0 / length) if freq == 0 else math.sqrt(2.0 / length)
        rows.append(factor * np.cos(freq * angles))
    for freq in range(1, kept // 2):
        rows.append(math.sqrt(2.0 / length) * np.sin(freq * angles))
    return np.stack(rows)


def node_of(index, axis, value):
    out = list(index)
    out[axis] = value
    return 25 * out[0] + 5 * out[1] + out[2]


def solver_tables(slopes):
    own = np.zeros((512, 512))
    near = np.zeros((512, 192))
    pick = np.zeros((192, 512))
    for i1 in range(5):
        for i2 in range(5):
            for i3 in range(5):
                index = (i1, i2, i3)
                node = 25 * i1 + 5 * i2 + i3
                for d in range(3):
                    u = 125 * (1 + d)
                    for k in range(5):
                        other = node_of(index, d, k)
                        own[node, u + other] += -2.0 * slopes[index[d], k]
                        own[u + node, other] += -2.0 * slopes[index[d], k]
                    rest = [index[e] for e in range(3) if e != d]
                    face = 5 * rest[0] + rest[1]
                    low, high = 64 * d + face, 64 * d + 32 + face
                    if index[d] == 0:
                        own[node, u + node] -= FACE_GAIN
                        own[node, node] -= FACE_GAIN
                        own[u + node, u + node] -= FACE_GAIN
                        own[u + node, node] -= FACE_GAIN
                        near[node, low] = FACE_GAIN
                        near[u + node, low] = FACE_GAIN
                        pick[high, node] = 1.0
                        pick[high, u + node] = -1.0
                    if index[d] == 4:
                        own[node, u + node] += FACE_GAIN
                        own[node, node] -= FACE_GAIN
                        own[u + node, node] += FACE_GAIN
                        own[u + node, u + node] -= FACE_GAIN
                        near[node, high] = FACE_GAIN
                        near[u + node, high] = -FACE_GAIN
                        pick[low, node] = 1.0
                        pick[low, u + node] = 1.0
    return tuple(t.astype(np.float32) for t in (own, near, pick))


def tables():
    slopes, interp = gll_tables()
    own, near, pick = solver_tables(slopes.astype(np.float64))
    interp = interp.astype(np.float64)
    regrid = np.zeros((64, 128), np.float32)
    regrid[:, :125] = np.kron(np.kron(interp, interp), interp).astype(np.float32)
    joint = np.kron(fourier_table(64, KM), fourier_table(64, KM)).astype(np.float32)
    joint = joint.reshape(256, 16, 4, 16, 4).transpose(2, 4, 0, 1, 3).reshape(16, 256, 256)
    inverse = jnp.asarray(joint).astype(jnp.bfloat16)
    forward = jnp.asarray(joint.transpose(0, 2, 1).reshape(4096, 256)).astype(jnp.bfloat16)
    along_x = jnp.asarray(fourier_table(128, KM), dtype=jnp.float32).astype(jnp.bfloat16)
    along_x = along_x.astype(jnp.float32).reshape(-1)
    return own, near, pick, regrid, forward, inverse, along_x


def normal_tail(x):
    bell = jnp.exp2(x * x * (-0.5 * LOG2E))
    den = 1.0 + (0.3275911 * HALF_ROOT) * jnp.abs(x)
    t = pl.reciprocal(den, approx=True)
    t = t * (2.0 - den * t)
    poly = 0.5 * 1.061405429 * t - 0.5 * 1.453152027
    poly = poly * t + 0.5 * 1.421413741
    poly = poly * t - 0.5 * 0.284496736
    poly = poly * t + 0.5 * 0.254829592
    return poly * t * bell, bell


def dot_f32(a, b):
    return jnp.dot(a, b, precision=HIGHEST, preferred_element_type=jnp.float32)


def dot_bf16(a, b):
    return jnp.dot(a, b, preferred_element_type=jnp.float32)


def column(row):
    eye = lax.broadcasted_iota(jnp.int32, (64, 64), 0) == lax.broadcasted_iota(
        jnp.int32, (64, 64), 1
    )
    col = jnp.sum(jnp.where(eye, row, 0.0), axis=1, keepdims=True)
    return jnp.broadcast_to(col, (64, 256))


def step_kernel(
    state_h, damping_h, mask_h, gain_h, weight_h, pick_h, regrid_h, table_h, own_h, near_h, spec_h,
    fwd_h, inv_h,
    new_state, coef_all, grad_all,
    state, damping, mask, gain, weight, pick, regrid, table_x, own, near, spec, fwd, inv,
    q, sec, faces, halo, edge, sink, a, b, gcol, wcol, g_a, g_b, pre, slope,
    fwd_sum, sib_sum, parts, inbox, total, mixed,
    ax, ax_hi, ax_lo,
    load_sem, halo_s, halo_r, sib_s, sib_r, part_s, part_r, mix_s, mix_r, hop_s, hop_r, z_s, z_r,
):
    grp, gx, gy = lax.axis_index("grp"), lax.axis_index("gx"), lax.axis_index("gy")
    chip, core = lax.div(gx, 2), lax.rem(gx, 2)
    cx, cy = lax.div(chip, 4), lax.rem(chip, 4)
    zme = grp * 2 + gy
    sibling = gx + 1 - 2 * core

    along = [[lax.rem(c + step, 4) for step in range(4)] for c in (cx, cy)]

    def chip_at(k, sign):
        return along[0][sign * (k // 4) % 4] * 4 + along[1][sign * (k % 4) % 4]

    def z_at(k):
        zt = lax.rem(zme + k, ZPEERS)
        return {"grp": lax.div(zt, 2), "gy": lax.rem(zt, 2)}

    def hops(k):
        return min(k // 4, 4 - k // 4) + min(k % 4, 4 - k % 4)

    others = sorted(range(1, CHIPS), key=hops)
    far = others[::-1]
    z_far = (4, 3, 5, 2, 6, 1, 7)

    def each(lo, hi, f, unroll=1):
        def step(k, carry):
            f(k)
            return carry
        lax.fori_loop(lo, hi, step, 0, unroll=unroll)

    fwd_parts = [pl.ds(1024 * i, 1024) for i in range(4)]
    moves = [
        (state_h.at[pl.ds(0, 256)], state.at[pl.ds(0, 256)]),
        (regrid_h, regrid),
        (gain_h, gain),
        *((fwd_h.at[part], fwd.at[part]) for part in fwd_parts),
        (state_h.at[pl.ds(256, 744)], state.at[pl.ds(256, 744)]),
        (pick_h, pick),
        (table_h, table_x),
        (damping_h, damping),
        (mask_h, mask),
        (own_h, own),
        (near_h, near),
        (spec_h, spec),
        (weight_h, weight),
        (inv_h, inv),
    ]
    loads = [pltpu.make_async_copy(*m, load_sem.at[i]) for i, m in enumerate(moves)]
    for c in loads[:7]:
        c.start()

    barrier = pltpu.get_barrier_semaphore()

    def greet(target):
        pl.semaphore_signal(barrier, inc=1, device_id=target, device_id_type=MESH)

    for k in others:
        greet({"gx": 2 * chip_at(k, 1) + core})
    greet({"gx": sibling})
    greet({"gx": lax.rem(gx + 2 * core + 31, 32)})
    for k in z_far:
        greet(z_at(k))

    for c in loads[:3]:
        c.wait()
    for c in loads[7:]:
        c.start()
    q[0:128, 0:128] = state[pl.ds(0, 128, stride=2), :]
    q[0:128, 128:256] = state[pl.ds(1, 128, stride=2), :]
    a[...] = dot_f32(regrid[...], q[0:128, :]).astype(jnp.bfloat16).astype(jnp.float32)
    gcol[...] = column(gain[...])
    fwd_sum[...] = jnp.zeros_like(fwd_sum)
    g_b[...] = jnp.zeros_like(g_b)

    def halo_copy(stage, side):
        to = lax.rem(gx + (1, 31)[side], 32)
        return pltpu.make_async_remote_copy(
            src_ref=faces.at[stage, pl.ds(32 * side, 32)],
            dst_ref=halo.at[stage, side],
            send_sem=halo_s.at[stage, side],
            recv_sem=halo_r.at[stage, side],
            device_id={"gx": to},
            device_id_type=MESH,
        )

    def rows_of(m, r):
        return pl.ds(128 * r + 32 * m, 32)

    def sib_copy(phase, r):
        return pltpu.make_async_remote_copy(
            src_ref=fwd_sum.at[phase, 1 - core, r],
            dst_ref=sib_sum.at[phase, r],
            send_sem=sib_s.at[phase, r],
            recv_sem=sib_r.at[phase, r],
            device_id={"gx": sibling},
            device_id_type=MESH,
        )

    def part_copy(phase, r, k):
        return pltpu.make_async_remote_copy(
            src_ref=parts.at[phase, r, k],
            dst_ref=inbox.at[phase, r, k],
            send_sem=part_s.at[phase, r, k],
            recv_sem=part_r.at[phase, r, k],
            device_id={"gx": 2 * chip_at(k, 1) + core},
            device_id_type=MESH,
        )

    def expand(phase, r, k):
        base = chip_at(k, 1) * 128 + 8 * chip
        acc = jnp.zeros((32, 128), jnp.float32)
        for m in range(4):
            rows = pl.ds(32 * m, 32)
            acc = acc + table_x[base + 4 * core + m] * fwd_sum[phase, core, r, rows, :]
            acc = acc + table_x[base + 4 - 4 * core + m] * sib_sum[phase, r, rows, :]
        return acc

    def scatter(phase, r):
        sib_copy(phase, r).wait()
        for k in far:
            parts[phase, r, k] = expand(phase, r, k)
            part_copy(phase, r, k).start()
        total[phase, r] = expand(phase, r, 0)

    def gather_sum(phase, r):
        ref = (coef_all, grad_all)[phase]
        summed = total[phase, r]
        for k in others:
            part_copy(phase, r, k).wait_recv()
            summed = summed + inbox[phase, r, k]
        ref[pl.ds(zme, 1), pl.ds(32 * r, 32), :] = summed[None]

    def z_copy(phase, r, k):
        ref = (coef_all, grad_all)[phase].at[zme, pl.ds(32 * r, 32)]
        return pltpu.make_async_remote_copy(
            src_ref=ref,
            dst_ref=ref,
            send_sem=z_s.at[phase, r, k],
            recv_sem=z_r.at[phase, r, k],
            device_id=z_at(k),
            device_id_type=MESH,
        )

    def transform(phase, i, g, halves):
        points = pl.ds(pl.multiple_of(512 * i, 512), 512)
        both = dot_bf16(g[pl.ds(128 * halves[0], 128 * len(halves)), :], fwd[points, :])
        for n, r in enumerate(halves):
            rows = slice(128 * n, 128 * n + 128)
            fwd_sum[phase, 0, r] += both[rows, 0:128]
            fwd_sum[phase, 1, r] += both[rows, 128:256]

    def lift(j, g, side):
        for m in range(4):
            row = a[pl.ds(m * 16 + j, 1), :]
            for r in range(2):
                x = gcol[pl.ds(32 * r, 32), :] * row
                lifted = jnp.maximum(x, 0.0) - jnp.abs(x) * normal_tail(x)[0]
                g[rows_of(m, r), 256 * side : 256 * side + 256] = lifted.astype(jnp.bfloat16)

    for i in range(4):
        loads[3 + i].wait()

    def lift_four(i):
        lift(4 * i, g_a, 0)
        lift(4 * i + 1, g_a, 1)
        transform(0, lax.rem(2 * i + 7, 8), g_b, (0, 1))
        lift(4 * i + 2, g_b, 0)
        lift(4 * i + 3, g_b, 1)
        transform(0, 2 * i, g_a, (0, 1))

    each(0, 4, lift_four)
    transform(0, 7, g_b, (0, 1))

    pl.semaphore_wait(barrier, CHIPS - 1 + 2 + ZPEERS - 1)

    for r in range(2):
        sib_copy(0, r).start()
    lanes = lax.broadcasted_iota(jnp.int32, (32, 256), 1)
    ez = lax.rem(lanes, 16)

    def rates(stage, fields):
        for side in range(2):
            halo_copy(stage, side).wait_recv()
        ends = (gx == 0, gx == 31)
        for side in range(2):
            edge[pl.ds(32 * side, 32), :] = jnp.where(ends[side], 0.0, halo[stage, side])
        low, high = faces[stage, 64:96, :], faces[stage, 96:128, :]
        edge[64:96, :] = jnp.where(lanes < 16, 0.0, pltpu.roll(low, 16, 1))
        edge[96:128, :] = jnp.where(lanes >= 240, 0.0, pltpu.roll(high, 240, 1))
        low, high = faces[stage, 128:160, :], faces[stage, 160:192, :]
        edge[128:160, :] = jnp.where(ez == 0, 0.0, pltpu.roll(low, 1, 1))
        edge[160:192, :] = jnp.where(ez == 15, 0.0, pltpu.roll(high, 255, 1))
        rate = dot_f32(own[...], fields[...]) + dot_f32(near[...], edge[...])
        return rate - sink[...] * fields[...]

    for c in loads[7:14]:
        c.wait()
    q[128:500, 0:128] = state[pl.ds(256, 372, stride=2), :]
    q[128:500, 128:256] = state[pl.ds(257, 372, stride=2), :]
    q[500:512, :] = jnp.zeros((12, 256), jnp.float32)
    sink[...] = mask[...].astype(jnp.float32) * damping[...]
    faces[0] = dot_f32(pick[...], q[...])
    for side in range(2):
        halo_copy(0, side).start()
    for r in range(2):
        scatter(0, r)

    sec[...] = q[...] + TIME_STEP * rates(0, q)
    faces[1] = dot_f32(pick[...], sec[...])
    for side in range(2):
        halo_copy(1, side).start()

    for r in range(2):
        gather_sum(0, r)

    loads[14].wait()

    def mix(i, acc):
        for u in range(8):
            c = i * 8 + u
            row = coef_all[pl.ds(zme, 1), pl.ds(c, 1), :].reshape(1, 128)
            acc = acc + spec[c] * row
        return acc

    mixed[0, 0] = lax.fori_loop(0, 8, mix, jnp.zeros((64, 128), jnp.float32)).astype(jnp.bfloat16)

    def mix_copy(k):
        return pltpu.make_async_remote_copy(
            src_ref=mixed.at[0, 0],
            dst_ref=mixed.at[0, k],
            send_sem=mix_s.at[k],
            recv_sem=mix_r.at[k],
            device_id={"gx": 2 * chip_at(k, 1) + core},
            device_id_type=MESH,
        )

    def hop_copy(k):
        direct = hops(k) > 2
        return pltpu.make_async_remote_copy(
            src_ref=mixed.at[0, 0 if direct else k],
            dst_ref=mixed.at[1, k],
            send_sem=hop_s.at[k],
            recv_sem=hop_r.at[k],
            device_id={"gx": 2 * chip_at(k, 1) + 1 - core if direct else sibling},
            device_id_type=MESH,
        )

    for k in far:
        mix_copy(k).start()
        if hops(k) > 2:
            hop_copy(k).start()
    hop_copy(0).start()
    for r in range(2):
        for k in z_far:
            z_copy(0, r, k).start()

    done = 0.5 * (q[...] + sec[...] + TIME_STEP * rates(1, sec))
    new_state[pl.ds(0, 500, stride=2), :] = done[0:500, 0:128]
    new_state[pl.ds(1, 500, stride=2), :] = done[0:500, 128:256]
    b[...] = dot_f32(regrid[...], done[0:128, :]).astype(jnp.bfloat16).astype(jnp.float32)

    def add_modes(half, k, acc):
        base = chip_at(k, -1) * 128 + 4 * gx
        value = mixed[half, k].astype(jnp.float32)
        return tuple(acc[m] + table_x[base + m] * value for m in range(4))

    zeros = tuple(jnp.zeros((64, 128), jnp.float32) for unused in range(4))
    sums = add_modes(0, 0, zeros)
    for k in others:
        mix_copy(k).wait_recv()
        if hops(k) <= 2:
            hop_copy(k).start()
        sums = add_modes(0, k, sums)
    for m in range(4):
        for r in range(2):
            ax[pl.ds(core, 1), rows_of(m, r), :] = sums[m][None, 32 * r : 32 * r + 32]
    sums = zeros
    for k in (0, *others):
        hop_copy(k).wait_recv()
        sums = add_modes(1, k, sums)
    for m in range(4):
        for r in range(2):
            ax[pl.ds(1 - core, 1), rows_of(m, r), :] = sums[m][None, 32 * r : 32 * r + 32]
    for half in range(2):
        value = ax[half]
        high = value.astype(jnp.bfloat16)
        ax_hi[:, 128 * half : 128 * half + 128] = high
        ax_lo[:, 128 * half : 128 * half + 128] = (value - high.astype(jnp.float32)).astype(
            jnp.bfloat16
        )

    loads[15].wait()
    loads[16].wait()
    wcol[...] = column(weight[...])
    g_b[...] = jnp.zeros_like(g_b)

    def inverse(j, slot):
        pre[slot] = dot_bf16(ax_hi[...], inv[j]) + dot_bf16(ax_lo[...], inv[j])

    def back(j, slot, g, side):
        cols = slice(256 * side, 256 * side + 256)
        for m in range(4):
            acc = jnp.zeros((8, 256), jnp.float32)
            for r in range(2):
                rows = rows_of(m, r)
                x = pre[slot, rows, :]
                tail, bell = normal_tail(x)
                cdf = jnp.where(x >= 0.0, 1.0 - tail, tail)
                slope[slot, rows, :] = cdf + x * bell * GAUSS_NORM
                act = x * cdf * wcol[pl.ds(32 * r, 32), :]
                acc = acc + jnp.sum(act.reshape(4, 8, 256), axis=0)
            misfit = jnp.sum(acc, axis=0, keepdims=True) - b[pl.ds(m * 16 + j, 1), :]
            misfit = (2.0 * LOSS_SCALE) * misfit
            for r in range(2):
                rows = rows_of(m, r)
                value = misfit * wcol[pl.ds(32 * r, 32), :] * slope[slot, rows, :]
                g[rows, cols] = value.astype(jnp.bfloat16)

    def back_four(i):
        inverse(4 * i + 1, 1)
        back(4 * i, 0, g_a, 0)
        inverse(4 * i + 2, 0)
        back(4 * i + 1, 1, g_a, 1)
        transform(1, lax.rem(2 * i + 7, 8), g_b, (0, 1))
        inverse(4 * i + 3, 1)
        back(4 * i + 2, 0, g_b, 0)
        inverse(lax.rem(4 * i + 4, 16), 0)
        back(4 * i + 3, 1, g_b, 1)
        transform(1, 2 * i, g_a, (0, 1))

    inverse(0, 0)
    each(0, 4, back_four)
    transform(1, 7, g_b, (0, 1))

    for r in range(2):
        sib_copy(1, r).start()
    for r in range(2):
        scatter(1, r)
    for r in range(2):
        gather_sum(1, r)
        for k in z_far:
            z_copy(1, r, k).start()

    for k in others:
        for phase in range(2):
            for r in range(2):
                part_copy(phase, r, k).wait_send()
        mix_copy(k).wait_send()
    for k in range(CHIPS):
        hop_copy(k).wait_send()
    for stage in range(2):
        for side in range(2):
            halo_copy(stage, side).wait_send()
    for phase in range(2):
        for r in range(2):
            for k in z_far:
                z_copy(phase, r, k).wait()


def update_kernel(
    coef, grad, spec, one, two, state, new_spec, new_one, new_two, new_state,
    out_spec, out_one, out_two, sem,
):
    move = pltpu.make_async_copy(state, new_state, sem.at[0, 3])
    move.start()
    block = 8

    def chunk(i):
        rows = pl.ds(block * i, block)
        return [
            pltpu.make_async_copy(src.at[rows], dst.at[rows], sem.at[i, n])
            for n, (src, dst) in enumerate(
                ((out_spec, new_spec), (out_one, new_one), (out_two, new_two))
            )
        ]

    def run(i, carry):
        for n in range(block):
            c = block * i + n
            acc = coef[0, pl.ds(c, 1), :] * grad[0]
            for t in range(1, ZPEERS):
                acc = acc + coef[t, pl.ds(c, 1), :] * grad[t]
            m1 = BETA_ONE * one[c].astype(jnp.float32) + (1.0 - BETA_ONE) * acc
            m2 = BETA_TWO * two[c].astype(jnp.float32) + (1.0 - BETA_TWO) * acc * acc
            scaled = m2 * (1.0 / BIAS_TWO)
            den = scaled * lax.rsqrt(scaled) + EPSILON
            inverse = pl.reciprocal(den, approx=True)
            inverse = inverse * (2.0 - den * inverse)
            out_spec[c] = spec[c] - (LEARN_RATE / BIAS_ONE) * m1 * inverse
            out_one[c] = m1.astype(jnp.bfloat16)
            out_two[c] = m2.astype(jnp.bfloat16)
        for copy in chunk(i):
            copy.start()
        return carry

    lax.fori_loop(0, 64 // block, run, 0)
    for i in range(64 // block):
        for copy in chunk(i):
            copy.wait()
    move.wait()


def per_device(state, damping, mask, gain, weight, spectral, moment_one, moment_two):
    own, near, pick, regrid, forward, inverse, along_x = tables()
    f32, bf16 = jnp.float32, jnp.bfloat16
    vmem = pl.BlockSpec(memory_space=pltpu.VMEM)
    hbm = pl.BlockSpec(memory_space=pltpu.HBM)
    anywhere = pl.BlockSpec(memory_space=pl.ANY)
    spec_t = jnp.transpose(spectral, (1, 2, 0))
    dma = pltpu.SemaphoreType.DMA
    new_state, coef_all, grad_all = pl.pallas_call(
        step_kernel,
        out_shape=(
            jax.ShapeDtypeStruct((1000, 128), f32),
            jax.ShapeDtypeStruct((ZPEERS, 64, 128), f32),
            jax.ShapeDtypeStruct((ZPEERS, 64, 128), f32),
        ),
        in_specs=[hbm] * 13,
        out_specs=(vmem, vmem, vmem),
        scratch_shapes=[
            pltpu.VMEM((1000, 128), f32),
            pltpu.VMEM((1, 256), f32),
            pltpu.VMEM((1, 256), jnp.int32),
            pltpu.VMEM((1, 64), f32),
            pltpu.VMEM((1, 64), f32),
            pltpu.VMEM((192, 512), f32),
            pltpu.VMEM((64, 128), f32),
            pltpu.SMEM((2048,), f32),
            pltpu.VMEM((512, 512), f32),
            pltpu.VMEM((512, 192), f32),
            pltpu.VMEM((64, 64, 128), f32),
            pltpu.VMEM((4096, 256), bf16),
            pltpu.VMEM((16, 256, 256), bf16),
            pltpu.VMEM((512, 256), f32),
            pltpu.VMEM((512, 256), f32),
            pltpu.VMEM((2, 192, 256), f32),
            pltpu.VMEM((2, 2, 32, 256), f32),
            pltpu.VMEM((192, 256), f32),
            pltpu.VMEM((1, 256), f32),
            pltpu.VMEM((64, 256), f32),
            pltpu.VMEM((64, 256), f32),
            pltpu.VMEM((64, 256), f32),
            pltpu.VMEM((64, 256), f32),
            pltpu.VMEM((256, 512), bf16),
            pltpu.VMEM((256, 512), bf16),
            pltpu.VMEM((2, 256, 256), f32),
            pltpu.VMEM((2, 256, 256), f32),
            pltpu.VMEM((2, 2, 2, 128, 128), f32),
            pltpu.VMEM((2, 2, 128, 128), f32),
            pltpu.VMEM((2, 2, CHIPS, 32, 128), f32),
            pltpu.VMEM((2, 2, CHIPS, 32, 128), f32),
            pltpu.VMEM((2, 2, 32, 128), f32),
            pltpu.VMEM((2, CHIPS, 64, 128), bf16),
            pltpu.VMEM((2, 256, 128), f32),
            pltpu.VMEM((256, 256), bf16),
            pltpu.VMEM((256, 256), bf16),
            dma((17,)),
            dma((2, 2)),
            dma((2, 2)),
            dma((2, 2)),
            dma((2, 2)),
            dma((2, 2, CHIPS)),
            dma((2, 2, CHIPS)),
            dma((CHIPS,)),
            dma((CHIPS,)),
            dma((CHIPS,)),
            dma((CHIPS,)),
            dma((2, 2, ZPEERS)),
            dma((2, 2, ZPEERS)),
        ],
        compiler_params=pltpu.CompilerParams(
            collective_id=0, has_side_effects=True, vmem_limit_bytes=40 * 1024 * 1024
        ),
        name="step",
    )(
        *(
            pltpu.with_memory_space_constraint(v, pltpu.HBM)
            for v in (
                state.reshape(1000, 128), damping, mask, gain.reshape(1, 64), weight.reshape(1, 64),
                pick, regrid, along_x, own, near, spec_t, forward, inverse,
            )
        )
    )
    new_spec, new_one, new_two, new_state = pl.pallas_call(
        update_kernel,
        out_shape=(
            jax.ShapeDtypeStruct((64, 64, 128), f32),
            jax.ShapeDtypeStruct((64, 64, 128), bf16),
            jax.ShapeDtypeStruct((64, 64, 128), bf16),
            jax.ShapeDtypeStruct((1000, 128), f32),
        ),
        in_specs=[vmem] * 5 + [anywhere],
        out_specs=(anywhere,) * 4,
        scratch_shapes=[
            pltpu.VMEM((64, 64, 128), f32),
            pltpu.VMEM((64, 64, 128), bf16),
            pltpu.VMEM((64, 64, 128), bf16),
            dma((8, 4)),
        ],
        compiler_params=pltpu.CompilerParams(vmem_limit_bytes=16 * 1024 * 1024),
        name="update",
    )(
        coef_all, grad_all, spec_t,
        jnp.transpose(moment_one, (1, 2, 0)), jnp.transpose(moment_two, (1, 2, 0)), new_state,
    )
    back = (2, 0, 1)
    return (
        new_state.reshape(state.shape),
        jnp.transpose(new_spec, back),
        jnp.transpose(new_one, back),
        jnp.transpose(new_two, back),
    )


def solution(mesh):
    in_specs = (
        P(("grp", "gy"), None, None, "gx", None),
        P("gx", None),
        P("gx", None),
        P(),
        P(),
        P("gx", None, None),
        P("gx", None, None),
        P("gx", None, None),
    )
    out_specs = (
        P(("grp", "gy"), None, None, "gx", None),
        P("gx", None, None),
        P("gx", None, None),
        P("gx", None, None),
    )
    return jax.shard_map(
        per_device, mesh=mesh, in_specs=in_specs, out_specs=out_specs, check_vma=False
    )
```

```python
import math

import jax
import jax.numpy as jnp
import numpy as np
from jax import lax
from jax.experimental import pallas as pl
from jax.experimental.pallas import tpu as pltpu
from jax.sharding import PartitionSpec as P

MESH = pl.DeviceIdType.MESH
HIGHEST = lax.Precision.HIGHEST
KM = 16
CHIPS = 16
ZPEERS = 8
PIECES = (((0, 64),), ((0, 32), (32, 32)))
TIME_STEP = 0.02
FACE_GAIN = 10.0
LOSS_SCALE = 1.0 / 2048.0
LEARN_RATE = 0.001
BETA_ONE = 0.9
BETA_TWO = 0.999
BIAS_ONE = 1.0 - BETA_ONE**10
BIAS_TWO = 1.0 - BETA_TWO**10
EPSILON = 1e-08
HALF_ROOT = 1.0 / math.sqrt(2.0)
GAUSS_NORM = 1.0 / math.sqrt(2.0 * math.pi)
LOG2E = 1.4426950408889634


def lagrange(nodes, column, point):
    value = 1.0
    for other in range(len(nodes)):
        if other != column:
            value = value * (point - nodes[other]) / (nodes[column] - nodes[other])
    return value


def lagrange_slope(nodes, column, point):
    total = 0.0
    for skipped in range(len(nodes)):
        if skipped != column:
            factor = 1.0 / (nodes[column] - nodes[skipped])
            for other in range(len(nodes)):
                if other != column and other != skipped:
                    factor = factor * (point - nodes[other]) / (nodes[column] - nodes[other])
            total = total + factor
    return total


def gll_tables():
    nodes = [-1.0, -math.sqrt(3.0 / 7.0), 0.0, math.sqrt(3.0 / 7.0), 1.0]
    slopes = np.array([[lagrange_slope(nodes, c, nodes[r]) for c in range(5)] for r in range(5)])
    interp = np.array(
        [[lagrange(nodes, c, -1.0 + (2.0 * m + 1.0) / 4.0) for c in range(5)] for m in range(4)]
    )
    return slopes.astype(np.float32), interp.astype(np.float32)


def fourier_table(length, kept):
    angles = np.arange(length) * (2.0 * math.pi / length)
    rows = []
    for freq in range(kept // 2 + 1):
        factor = math.sqrt(1.0 / length) if freq == 0 else math.sqrt(2.0 / length)
        rows.append(factor * np.cos(freq * angles))
    for freq in range(1, kept // 2):
        rows.append(math.sqrt(2.0 / length) * np.sin(freq * angles))
    return np.stack(rows)


def node_of(index, axis, value):
    out = list(index)
    out[axis] = value
    return 25 * out[0] + 5 * out[1] + out[2]


def solver_tables(slopes):
    own = np.zeros((512, 512))
    near = np.zeros((512, 192))
    pick = np.zeros((192, 512))
    for i1 in range(5):
        for i2 in range(5):
            for i3 in range(5):
                index = (i1, i2, i3)
                node = 25 * i1 + 5 * i2 + i3
                for d in range(3):
                    u = 125 * (1 + d)
                    for k in range(5):
                        other = node_of(index, d, k)
                        own[node, u + other] += -2.0 * slopes[index[d], k]
                        own[u + node, other] += -2.0 * slopes[index[d], k]
                    rest = [index[e] for e in range(3) if e != d]
                    face = 5 * rest[0] + rest[1]
                    low, high = 64 * d + face, 64 * d + 32 + face
                    if index[d] == 0:
                        own[node, u + node] -= FACE_GAIN
                        own[node, node] -= FACE_GAIN
                        own[u + node, u + node] -= FACE_GAIN
                        own[u + node, node] -= FACE_GAIN
                        near[node, low] = FACE_GAIN
                        near[u + node, low] = FACE_GAIN
                        pick[high, node] = 1.0
                        pick[high, u + node] = -1.0
                    if index[d] == 4:
                        own[node, u + node] += FACE_GAIN
                        own[node, node] -= FACE_GAIN
                        own[u + node, node] += FACE_GAIN
                        own[u + node, u + node] -= FACE_GAIN
                        near[node, high] = FACE_GAIN
                        near[u + node, high] = -FACE_GAIN
                        pick[low, node] = 1.0
                        pick[low, u + node] = 1.0
    return tuple(t.astype(np.float32) for t in (own, near, pick))


def tables():
    slopes, interp = gll_tables()
    own, near, pick = solver_tables(slopes.astype(np.float64))
    interp = interp.astype(np.float64)
    regrid = np.zeros((64, 128), np.float32)
    regrid[:, :125] = np.kron(np.kron(interp, interp), interp).astype(np.float32)
    joint = np.kron(fourier_table(64, KM), fourier_table(64, KM)).astype(np.float32)
    joint = joint.reshape(256, 16, 4, 16, 4).transpose(2, 4, 0, 1, 3).reshape(16, 256, 256)
    inverse = jnp.asarray(joint).astype(jnp.bfloat16)
    forward = jnp.asarray(joint.transpose(0, 2, 1).reshape(4096, 256)).astype(jnp.bfloat16)
    along_x = jnp.asarray(fourier_table(128, KM), dtype=jnp.float32).astype(jnp.bfloat16)
    along_x = along_x.astype(jnp.float32).reshape(-1)
    return own, near, pick, regrid, forward, inverse, along_x


def normal_cdf(x):
    return 0.5 + 0.5 * lax.erf(x * HALF_ROOT)


def dot_f32(a, b):
    return jnp.dot(a, b, precision=HIGHEST, preferred_element_type=jnp.float32)


def dot_bf16(a, b):
    return jnp.dot(a, b, preferred_element_type=jnp.float32)


def column(row):
    eye = lax.broadcasted_iota(jnp.int32, (64, 64), 0) == lax.broadcasted_iota(
        jnp.int32, (64, 64), 1
    )
    col = jnp.sum(jnp.where(eye, row, 0.0), axis=1, keepdims=True)
    return jnp.broadcast_to(col, (64, 256))


def step_kernel(
    state_h, damping_h, mask_h, gain_h, weight_h, pick_h, regrid_h, table_h, own_h, near_h, spec_h,
    fwd_h, inv_h,
    new_state, coef_all, grad_all,
    state, damping, mask, gain, weight, pick, regrid, table_x, own, near, spec, fwd, inv,
    q, sec, faces, halo, edge, sink, a, b, gcol, wcol, g_a, g_b, pre, slope,
    fwd_sum, sib_sum, parts, inbox, total, mixed,
    ax, ax_hi, ax_lo,
    load_sem, halo_s, halo_r, sib_s, sib_r, part_s, part_r, mix_s, mix_r, hop_s, hop_r, z_s, z_r,
):
    grp, gx, gy = lax.axis_index("grp"), lax.axis_index("gx"), lax.axis_index("gy")
    chip, core = lax.div(gx, 2), lax.rem(gx, 2)
    cx, cy = lax.div(chip, 4), lax.rem(chip, 4)
    zme = grp * 2 + gy
    sibling = gx + 1 - 2 * core

    along = [[lax.rem(c + step, 4) for step in range(4)] for c in (cx, cy)]

    def chip_at(k, sign):
        return along[0][sign * (k // 4) % 4] * 4 + along[1][sign * (k % 4) % 4]

    def z_at(k):
        zt = lax.rem(zme + k, ZPEERS)
        return {"grp": lax.div(zt, 2), "gy": lax.rem(zt, 2)}

    def hops(k):
        return min(k // 4, 4 - k // 4) + min(k % 4, 4 - k % 4)

    others = sorted(range(1, CHIPS), key=hops)
    far = others[::-1]
    z_far = (4, 3, 5, 2, 6, 1, 7)

    def each(lo, hi, f, unroll=1):
        def step(k, carry):
            f(k)
            return carry
        lax.fori_loop(lo, hi, step, 0, unroll=unroll)

    fwd_parts = [pl.ds(1024 * i, 1024) for i in range(4)]
    moves = [
        (state_h.at[pl.ds(0, 256)], state.at[pl.ds(0, 256)]),
        (regrid_h, regrid),
        (gain_h, gain),
        *((fwd_h.at[part], fwd.at[part]) for part in fwd_parts),
        (state_h.at[pl.ds(256, 744)], state.at[pl.ds(256, 744)]),
        (pick_h, pick),
        (table_h, table_x),
        (damping_h, damping),
        (mask_h, mask),
        (own_h, own),
        (near_h, near),
        (spec_h, spec),
        (weight_h, weight),
        (inv_h, inv),
    ]
    loads = [pltpu.make_async_copy(*m, load_sem.at[i]) for i, m in enumerate(moves)]
    for c in loads[:7]:
        c.start()

    barrier = pltpu.get_barrier_semaphore()

    def greet(target):
        pl.semaphore_signal(barrier, inc=1, device_id=target, device_id_type=MESH)

    for k in others:
        greet({"gx": 2 * chip_at(k, 1) + core})
    greet({"gx": sibling})
    greet({"gx": lax.rem(gx + 2 * core + 31, 32)})
    for k in z_far:
        greet(z_at(k))

    for c in loads[:3]:
        c.wait()
    for c in loads[7:]:
        c.start()
    q[0:128, 0:128] = state[pl.ds(0, 128, stride=2), :]
    q[0:128, 128:256] = state[pl.ds(1, 128, stride=2), :]
    a[...] = dot_f32(regrid[...], q[0:128, :]).astype(jnp.bfloat16).astype(jnp.float32)
    gcol[...] = column(gain[...])
    fwd_sum[...] = jnp.zeros_like(fwd_sum)
    g_b[...] = jnp.zeros_like(g_b)

    def halo_copy(stage, side):
        to = lax.rem(gx + (1, 31)[side], 32)
        return pltpu.make_async_remote_copy(
            src_ref=faces.at[stage, pl.ds(32 * side, 32)],
            dst_ref=halo.at[stage, side],
            send_sem=halo_s.at[stage, side],
            recv_sem=halo_r.at[stage, side],
            device_id={"gx": to},
            device_id_type=MESH,
        )

    def rows_of(m, r):
        return pl.ds(128 * r + 32 * m, 32)

    def sib_copy(phase, r):
        return pltpu.make_async_remote_copy(
            src_ref=fwd_sum.at[phase, 1 - core, r],
            dst_ref=sib_sum.at[phase, r],
            send_sem=sib_s.at[phase, r],
            recv_sem=sib_r.at[phase, r],
            device_id={"gx": sibling},
            device_id_type=MESH,
        )

    def piece(phase, n):
        first, count = PIECES[phase][n]
        return first, count, pl.ds(first, count)

    def part_copy(phase, n, k):
        rows = piece(phase, n)[2]
        return pltpu.make_async_remote_copy(
            src_ref=parts.at[phase, k, rows],
            dst_ref=inbox.at[phase, k, rows],
            send_sem=part_s.at[phase, n, k],
            recv_sem=part_r.at[phase, n, k],
            device_id={"gx": 2 * chip_at(k, 1) + core},
            device_id_type=MESH,
        )

    def expand(phase, n, k, whose):
        base = chip_at(k, 1) * 128 + 8 * chip + (4 * core if whose == 0 else 4 - 4 * core)
        first, count, unused = piece(phase, n)
        sums = []
        for r in range(first // 32, -(-(first + count) // 32)):
            acc = jnp.zeros((32, 128), jnp.float32)
            for m in range(4):
                rows = pl.ds(32 * m, 32)
                value = (
                    fwd_sum[phase, core, r, rows, :] if whose == 0 else sib_sum[phase, r, rows, :]
                )
                acc = acc + table_x[base + m] * value
            sums.append(acc)
        return sums[0] if len(sums) == 1 else jnp.concatenate(sums, axis=0)

    def prepare(phase, n):
        rows = piece(phase, n)[2]
        for k in (*far, 0):
            parts[phase, k, rows, :] = expand(phase, n, k, 0)

    def scatter(phase, n):
        rows = piece(phase, n)[2]
        for k in far:
            parts[phase, k, rows, :] += expand(phase, n, k, 1)
            part_copy(phase, n, k).start()
        total[phase, rows, :] = parts[phase, 0, rows, :] + expand(phase, n, 0, 1)

    def gather_sum(phase, n):
        rows = piece(phase, n)[2]
        ref = (coef_all, grad_all)[phase]
        summed = total[phase, rows, :]
        for k in others:
            part_copy(phase, n, k).wait_recv()
            summed = summed + inbox[phase, k, rows, :]
        ref[pl.ds(zme, 1), rows, :] = summed[None]

    def z_copy(phase, n, k):
        ref = (coef_all, grad_all)[phase].at[zme, piece(phase, n)[2]]
        return pltpu.make_async_remote_copy(
            src_ref=ref,
            dst_ref=ref,
            send_sem=z_s.at[phase, n, k],
            recv_sem=z_r.at[phase, n, k],
            device_id=z_at(k),
            device_id_type=MESH,
        )

    def transform(phase, i, g, halves):
        points = pl.ds(pl.multiple_of(512 * i, 512), 512)
        both = dot_bf16(g[pl.ds(128 * halves[0], 128 * len(halves)), :], fwd[points, :])
        for n, r in enumerate(halves):
            rows = slice(128 * n, 128 * n + 128)
            fwd_sum[phase, 0, r] += both[rows, 0:128]
            fwd_sum[phase, 1, r] += both[rows, 128:256]

    def lift(j, g, side):
        for m in range(4):
            row = a[pl.ds(m * 16 + j, 1), :]
            for r in range(2):
                x = gcol[pl.ds(32 * r, 32), :] * row
                lifted = x * normal_cdf(x)
                g[rows_of(m, r), 256 * side : 256 * side + 256] = lifted.astype(jnp.bfloat16)

    for i in range(4):
        loads[3 + i].wait()

    def lift_four(i):
        lift(4 * i, g_a, 0)
        lift(4 * i + 1, g_a, 1)
        transform(0, lax.rem(2 * i + 7, 8), g_b, (0, 1))
        lift(4 * i + 2, g_b, 0)
        lift(4 * i + 3, g_b, 1)
        transform(0, 2 * i, g_a, (0, 1))

    each(0, 4, lift_four)
    transform(0, 7, g_b, (0, 1))

    pl.semaphore_wait(barrier, CHIPS - 1 + 2 + ZPEERS - 1)

    for r in range(2):
        sib_copy(0, r).start()

    lanes = lax.broadcasted_iota(jnp.int32, (32, 256), 1)
    ez = lax.rem(lanes, 16)

    def rates(stage, fields):
        for side in range(2):
            halo_copy(stage, side).wait_recv()
        ends = (gx == 0, gx == 31)
        for side in range(2):
            edge[pl.ds(32 * side, 32), :] = jnp.where(ends[side], 0.0, halo[stage, side])
        low, high = faces[stage, 64:96, :], faces[stage, 96:128, :]
        edge[64:96, :] = jnp.where(lanes < 16, 0.0, pltpu.roll(low, 16, 1))
        edge[96:128, :] = jnp.where(lanes >= 240, 0.0, pltpu.roll(high, 240, 1))
        low, high = faces[stage, 128:160, :], faces[stage, 160:192, :]
        edge[128:160, :] = jnp.where(ez == 0, 0.0, pltpu.roll(low, 1, 1))
        edge[160:192, :] = jnp.where(ez == 15, 0.0, pltpu.roll(high, 255, 1))
        rate = dot_f32(own[...], fields[...]) + dot_f32(near[...], edge[...])
        return rate - sink[...] * fields[...]

    for c in loads[7:14]:
        c.wait()
    q[128:500, 0:128] = state[pl.ds(256, 372, stride=2), :]
    q[128:500, 128:256] = state[pl.ds(257, 372, stride=2), :]
    q[500:512, :] = jnp.zeros((12, 256), jnp.float32)
    sink[...] = mask[...].astype(jnp.float32) * damping[...]
    faces[0, 0:64] = dot_f32(pick[0:64, :], q[...])
    for side in range(2):
        halo_copy(0, side).start()
    prepare(0, 0)
    for r in range(2):
        sib_copy(0, r).wait()
    scatter(0, 0)
    faces[0, 64:192] = dot_f32(pick[64:192, :], q[...])

    sec[...] = q[...] + TIME_STEP * rates(0, q)
    faces[1] = dot_f32(pick[...], sec[...])
    for side in range(2):
        halo_copy(1, side).start()

    for n in range(len(PIECES[0])):
        gather_sum(0, n)

    loads[14].wait()

    def mix(i, acc):
        for u in range(8):
            c = i * 8 + u
            row = coef_all[pl.ds(zme, 1), pl.ds(c, 1), :].reshape(1, 128)
            acc = acc + spec[c] * row
        return acc

    mixed[0, 0] = lax.fori_loop(0, 8, mix, jnp.zeros((64, 128), jnp.float32)).astype(jnp.bfloat16)

    def mix_copy(k):
        return pltpu.make_async_remote_copy(
            src_ref=mixed.at[0, 0],
            dst_ref=mixed.at[0, k],
            send_sem=mix_s.at[k],
            recv_sem=mix_r.at[k],
            device_id={"gx": 2 * chip_at(k, 1) + core},
            device_id_type=MESH,
        )

    def hop_copy(k):
        direct = hops(k) > 2
        return pltpu.make_async_remote_copy(
            src_ref=mixed.at[0, 0 if direct else k],
            dst_ref=mixed.at[1, k],
            send_sem=hop_s.at[k],
            recv_sem=hop_r.at[k],
            device_id={"gx": 2 * chip_at(k, 1) + 1 - core if direct else sibling},
            device_id_type=MESH,
        )

    for k in far:
        mix_copy(k).start()
        if hops(k) > 2:
            hop_copy(k).start()
    hop_copy(0).start()
    for n in range(len(PIECES[0])):
        for k in z_far:
            z_copy(0, n, k).start()

    done = 0.5 * (q[...] + sec[...] + TIME_STEP * rates(1, sec))
    new_state[pl.ds(0, 500, stride=2), :] = done[0:500, 0:128]
    new_state[pl.ds(1, 500, stride=2), :] = done[0:500, 128:256]
    b[...] = dot_f32(regrid[...], done[0:128, :]).astype(jnp.bfloat16).astype(jnp.float32)

    def add_modes(half, k, acc):
        base = chip_at(k, -1) * 128 + 4 * gx
        value = mixed[half, k].astype(jnp.float32)
        return tuple(acc[m] + table_x[base + m] * value for m in range(4))

    zeros = tuple(jnp.zeros((64, 128), jnp.float32) for unused in range(4))
    sums = add_modes(0, 0, zeros)
    for k in others:
        mix_copy(k).wait_recv()
        if hops(k) <= 2:
            hop_copy(k).start()
        sums = add_modes(0, k, sums)
    for m in range(4):
        for r in range(2):
            ax[pl.ds(core, 1), rows_of(m, r), :] = sums[m][None, 32 * r : 32 * r + 32]
    sums = zeros
    for k in (0, *others):
        hop_copy(k).wait_recv()
        sums = add_modes(1, k, sums)
    for m in range(4):
        for r in range(2):
            ax[pl.ds(1 - core, 1), rows_of(m, r), :] = sums[m][None, 32 * r : 32 * r + 32]
    for half in range(2):
        value = ax[half]
        high = value.astype(jnp.bfloat16)
        ax_hi[:, 128 * half : 128 * half + 128] = high
        ax_lo[:, 128 * half : 128 * half + 128] = (value - high.astype(jnp.float32)).astype(
            jnp.bfloat16
        )

    loads[15].wait()
    loads[16].wait()
    wcol[...] = column(weight[...])
    g_b[...] = jnp.zeros_like(g_b)

    def inverse(j, slot):
        pre[slot] = dot_bf16(ax_hi[...], inv[j]) + dot_bf16(ax_lo[...], inv[j])

    def back(j, slot, g, side):
        cols = slice(256 * side, 256 * side + 256)
        for m in range(4):
            acc = jnp.zeros((8, 256), jnp.float32)
            for r in range(2):
                rows = rows_of(m, r)
                x = pre[slot, rows, :]
                cdf = normal_cdf(x)
                bell = jnp.exp2(x * x * (-0.5 * LOG2E))
                slope[slot, rows, :] = cdf + x * bell * GAUSS_NORM
                act = x * cdf * wcol[pl.ds(32 * r, 32), :]
                acc = acc + jnp.sum(act.reshape(4, 8, 256), axis=0)
            misfit = jnp.sum(acc, axis=0, keepdims=True) - b[pl.ds(m * 16 + j, 1), :]
            misfit = (2.0 * LOSS_SCALE) * misfit
            for r in range(2):
                rows = rows_of(m, r)
                value = misfit * wcol[pl.ds(32 * r, 32), :] * slope[slot, rows, :]
                g[rows, cols] = value.astype(jnp.bfloat16)

    def back_four(i):
        inverse(4 * i + 1, 1)
        back(4 * i, 0, g_a, 0)
        inverse(4 * i + 2, 0)
        back(4 * i + 1, 1, g_a, 1)
        transform(1, lax.rem(2 * i + 7, 8), g_b, (0, 1))
        inverse(4 * i + 3, 1)
        back(4 * i + 2, 0, g_b, 0)
        inverse(lax.rem(4 * i + 4, 16), 0)
        back(4 * i + 3, 1, g_b, 1)
        transform(1, 2 * i, g_a, (0, 1))

    inverse(0, 0)
    each(0, 4, back_four)
    transform(1, 7, g_b, (0, 1))

    for r in range(2):
        sib_copy(1, r).start()
    for n in range(2):
        prepare(1, n)
    for n in range(2):
        sib_copy(1, n).wait()
        scatter(1, n)
    for n in range(len(PIECES[1])):
        gather_sum(1, n)
        for k in z_far:
            z_copy(1, n, k).start()

    for k in others:
        for phase in range(2):
            for n in range(len(PIECES[phase])):
                part_copy(phase, n, k).wait_send()
        mix_copy(k).wait_send()
    for k in range(CHIPS):
        hop_copy(k).wait_send()
    for stage in range(2):
        for side in range(2):
            halo_copy(stage, side).wait_send()
    for phase in range(2):
        for n in range(len(PIECES[phase])):
            for k in z_far:
                z_copy(phase, n, k).wait()


def update_kernel(
    coef, grad, spec, one, two, state, new_spec, new_one, new_two, new_state,
    out_spec, out_one, out_two, sem,
):
    move = pltpu.make_async_copy(state, new_state, sem.at[0, 3])
    move.start()
    block = 8

    def chunk(i):
        rows = pl.ds(block * i, block)
        return [
            pltpu.make_async_copy(src.at[rows], dst.at[rows], sem.at[i, n])
            for n, (src, dst) in enumerate(
                ((out_spec, new_spec), (out_one, new_one), (out_two, new_two))
            )
        ]

    def run(i, carry):
        for n in range(block):
            c = block * i + n
            acc = coef[0, pl.ds(c, 1), :] * grad[0]
            for t in range(1, ZPEERS):
                acc = acc + coef[t, pl.ds(c, 1), :] * grad[t]
            m1 = BETA_ONE * one[c].astype(jnp.float32) + (1.0 - BETA_ONE) * acc
            m2 = BETA_TWO * two[c].astype(jnp.float32) + (1.0 - BETA_TWO) * acc * acc
            scaled = m2 * (1.0 / BIAS_TWO)
            den = scaled * lax.rsqrt(scaled) + EPSILON
            inverse = 1.0 / den
            out_spec[c] = spec[c] - (LEARN_RATE / BIAS_ONE) * m1 * inverse
            out_one[c] = m1.astype(jnp.bfloat16)
            out_two[c] = m2.astype(jnp.bfloat16)
        for copy in chunk(i):
            copy.start()
        return carry

    lax.fori_loop(0, 64 // block, run, 0)
    for i in range(64 // block):
        for copy in chunk(i):
            copy.wait()
    move.wait()


def per_device(state, damping, mask, gain, weight, spectral, moment_one, moment_two):
    own, near, pick, regrid, forward, inverse, along_x = tables()
    f32, bf16 = jnp.float32, jnp.bfloat16
    vmem = pl.BlockSpec(memory_space=pltpu.VMEM)
    hbm = pl.BlockSpec(memory_space=pltpu.HBM)
    anywhere = pl.BlockSpec(memory_space=pl.ANY)
    spec_t = jnp.transpose(spectral, (1, 2, 0))
    dma = pltpu.SemaphoreType.DMA
    new_state, coef_all, grad_all = pl.pallas_call(
        step_kernel,
        out_shape=(
            jax.ShapeDtypeStruct((1000, 128), f32),
            jax.ShapeDtypeStruct((ZPEERS, 64, 128), f32),
            jax.ShapeDtypeStruct((ZPEERS, 64, 128), f32),
        ),
        in_specs=[hbm] * 13,
        out_specs=(vmem, vmem, vmem),
        scratch_shapes=[
            pltpu.VMEM((1000, 128), f32),
            pltpu.VMEM((1, 256), f32),
            pltpu.VMEM((1, 256), jnp.int32),
            pltpu.VMEM((1, 64), f32),
            pltpu.VMEM((1, 64), f32),
            pltpu.VMEM((192, 512), f32),
            pltpu.VMEM((64, 128), f32),
            pltpu.SMEM((2048,), f32),
            pltpu.VMEM((512, 512), f32),
            pltpu.VMEM((512, 192), f32),
            pltpu.VMEM((64, 64, 128), f32),
            pltpu.VMEM((4096, 256), bf16),
            pltpu.VMEM((16, 256, 256), bf16),
            pltpu.VMEM((512, 256), f32),
            pltpu.VMEM((512, 256), f32),
            pltpu.VMEM((2, 192, 256), f32),
            pltpu.VMEM((2, 2, 32, 256), f32),
            pltpu.VMEM((192, 256), f32),
            pltpu.VMEM((1, 256), f32),
            pltpu.VMEM((64, 256), f32),
            pltpu.VMEM((64, 256), f32),
            pltpu.VMEM((64, 256), f32),
            pltpu.VMEM((64, 256), f32),
            pltpu.VMEM((256, 512), bf16),
            pltpu.VMEM((256, 512), bf16),
            pltpu.VMEM((2, 256, 256), f32),
            pltpu.VMEM((2, 256, 256), f32),
            pltpu.VMEM((2, 2, 2, 128, 128), f32),
            pltpu.VMEM((2, 2, 128, 128), f32),
            pltpu.VMEM((2, CHIPS, 64, 128), f32),
            pltpu.VMEM((2, CHIPS, 64, 128), f32),
            pltpu.VMEM((2, 64, 128), f32),
            pltpu.VMEM((2, CHIPS, 64, 128), bf16),
            pltpu.VMEM((2, 256, 128), f32),
            pltpu.VMEM((256, 256), bf16),
            pltpu.VMEM((256, 256), bf16),
            dma((17,)),
            dma((2, 2)),
            dma((2, 2)),
            dma((2, 2)),
            dma((2, 2)),
            dma((2, 2, CHIPS)),
            dma((2, 2, CHIPS)),
            dma((CHIPS,)),
            dma((CHIPS,)),
            dma((CHIPS,)),
            dma((CHIPS,)),
            dma((2, 2, ZPEERS)),
            dma((2, 2, ZPEERS)),
        ],
        compiler_params=pltpu.CompilerParams(
            collective_id=0, has_side_effects=True, vmem_limit_bytes=40 * 1024 * 1024
        ),
        name="step",
    )(
        *(
            pltpu.with_memory_space_constraint(v, pltpu.HBM)
            for v in (
                state.reshape(1000, 128), damping, mask, gain.reshape(1, 64), weight.reshape(1, 64),
                pick, regrid, along_x, own, near, spec_t, forward, inverse,
            )
        )
    )
    new_spec, new_one, new_two, new_state = pl.pallas_call(
        update_kernel,
        out_shape=(
            jax.ShapeDtypeStruct((64, 64, 128), f32),
            jax.ShapeDtypeStruct((64, 64, 128), bf16),
            jax.ShapeDtypeStruct((64, 64, 128), bf16),
            jax.ShapeDtypeStruct((1000, 128), f32),
        ),
        in_specs=[vmem] * 5 + [anywhere],
        out_specs=(anywhere,) * 4,
        scratch_shapes=[
            pltpu.VMEM((64, 64, 128), f32),
            pltpu.VMEM((64, 64, 128), bf16),
            pltpu.VMEM((64, 64, 128), bf16),
            dma((8, 4)),
        ],
        compiler_params=pltpu.CompilerParams(vmem_limit_bytes=16 * 1024 * 1024),
        name="update",
    )(
        coef_all, grad_all, spec_t,
        jnp.transpose(moment_one, (1, 2, 0)), jnp.transpose(moment_two, (1, 2, 0)), new_state,
    )
    back = (2, 0, 1)
    return (
        new_state.reshape(state.shape),
        jnp.transpose(new_spec, back),
        jnp.transpose(new_one, back),
        jnp.transpose(new_two, back),
    )


def solution(mesh):
    in_specs = (
        P(("grp", "gy"), None, None, "gx", None),
        P("gx", None),
        P("gx", None),
        P(),
        P(),
        P("gx", None, None),
        P("gx", None, None),
        P("gx", None, None),
    )
    out_specs = (
        P(("grp", "gy"), None, None, "gx", None),
        P("gx", None, None),
        P("gx", None, None),
        P("gx", None, None),
    )
    return jax.shard_map(
        per_device, mesh=mesh, in_specs=in_specs, out_specs=out_specs, check_vma=False
    )
```

```python
import math

import jax
import jax.numpy as jnp
import numpy as np
from jax import lax
from jax.experimental import pallas as pl
from jax.experimental.pallas import tpu as pltpu
from jax.sharding import PartitionSpec as P

MESH = pl.DeviceIdType.MESH
HIGHEST = lax.Precision.HIGHEST
KM = 16
CHIPS = 16
ZPEERS = 8
PIECES = (((0, 64),), ((0, 32), (32, 32)))
TIME_STEP = 0.02
FACE_GAIN = 10.0
LOSS_SCALE = 1.0 / 2048.0
LEARN_RATE = 0.001
BETA_ONE = 0.9
BETA_TWO = 0.999
BIAS_ONE = 1.0 - BETA_ONE**10
BIAS_TWO = 1.0 - BETA_TWO**10
EPSILON = 1e-08
HALF_ROOT = 1.0 / math.sqrt(2.0)
GAUSS_NORM = 1.0 / math.sqrt(2.0 * math.pi)
LOG2E = 1.4426950408889634


def lagrange(nodes, column, point):
    value = 1.0
    for other in range(len(nodes)):
        if other != column:
            value = value * (point - nodes[other]) / (nodes[column] - nodes[other])
    return value


def lagrange_slope(nodes, column, point):
    total = 0.0
    for skipped in range(len(nodes)):
        if skipped != column:
            factor = 1.0 / (nodes[column] - nodes[skipped])
            for other in range(len(nodes)):
                if other != column and other != skipped:
                    factor = factor * (point - nodes[other]) / (nodes[column] - nodes[other])
            total = total + factor
    return total


def gll_tables():
    nodes = [-1.0, -math.sqrt(3.0 / 7.0), 0.0, math.sqrt(3.0 / 7.0), 1.0]
    slopes = np.array([[lagrange_slope(nodes, c, nodes[r]) for c in range(5)] for r in range(5)])
    interp = np.array(
        [[lagrange(nodes, c, -1.0 + (2.0 * m + 1.0) / 4.0) for c in range(5)] for m in range(4)]
    )
    return slopes.astype(np.float32), interp.astype(np.float32)


def fourier_table(length, kept):
    angles = np.arange(length) * (2.0 * math.pi / length)
    rows = []
    for freq in range(kept // 2 + 1):
        factor = math.sqrt(1.0 / length) if freq == 0 else math.sqrt(2.0 / length)
        rows.append(factor * np.cos(freq * angles))
    for freq in range(1, kept // 2):
        rows.append(math.sqrt(2.0 / length) * np.sin(freq * angles))
    return np.stack(rows)


def node_of(index, axis, value):
    out = list(index)
    out[axis] = value
    return 25 * out[0] + 5 * out[1] + out[2]


def solver_tables(slopes):
    own = np.zeros((512, 512))
    near = np.zeros((512, 192))
    pick = np.zeros((192, 512))
    for i1 in range(5):
        for i2 in range(5):
            for i3 in range(5):
                index = (i1, i2, i3)
                node = 25 * i1 + 5 * i2 + i3
                for d in range(3):
                    u = 125 * (1 + d)
                    for k in range(5):
                        other = node_of(index, d, k)
                        own[node, u + other] += -2.0 * slopes[index[d], k]
                        own[u + node, other] += -2.0 * slopes[index[d], k]
                    rest = [index[e] for e in range(3) if e != d]
                    face = 5 * rest[0] + rest[1]
                    low, high = 64 * d + face, 64 * d + 32 + face
                    if index[d] == 0:
                        own[node, u + node] -= FACE_GAIN
                        own[node, node] -= FACE_GAIN
                        own[u + node, u + node] -= FACE_GAIN
                        own[u + node, node] -= FACE_GAIN
                        near[node, low] = FACE_GAIN
                        near[u + node, low] = FACE_GAIN
                        pick[high, node] = 1.0
                        pick[high, u + node] = -1.0
                    if index[d] == 4:
                        own[node, u + node] += FACE_GAIN
                        own[node, node] -= FACE_GAIN
                        own[u + node, node] += FACE_GAIN
                        own[u + node, u + node] -= FACE_GAIN
                        near[node, high] = FACE_GAIN
                        near[u + node, high] = -FACE_GAIN
                        pick[low, node] = 1.0
                        pick[low, u + node] = 1.0
    return tuple(t.astype(np.float32) for t in (own, near, pick))


def tables():
    slopes, interp = gll_tables()
    own, near, pick = solver_tables(slopes.astype(np.float64))
    interp = interp.astype(np.float64)
    regrid = np.zeros((64, 128), np.float32)
    regrid[:, :125] = np.kron(np.kron(interp, interp), interp).astype(np.float32)
    joint = np.kron(fourier_table(64, KM), fourier_table(64, KM)).astype(np.float32)
    joint = joint.reshape(256, 16, 4, 16, 4).transpose(2, 4, 0, 1, 3).reshape(16, 256, 256)
    inverse = jnp.asarray(joint).astype(jnp.bfloat16)
    forward = jnp.asarray(joint.transpose(0, 2, 1).reshape(4096, 256)).astype(jnp.bfloat16)
    along_x = jnp.asarray(fourier_table(128, KM), dtype=jnp.float32).astype(jnp.bfloat16)
    along_x = along_x.astype(jnp.float32).reshape(-1)
    return own, near, pick, regrid, forward, inverse, along_x


def normal_cdf(x):
    return 0.5 + 0.5 * lax.erf(x * HALF_ROOT)


def dot_f32(a, b):
    return jnp.dot(a, b, precision=HIGHEST, preferred_element_type=jnp.float32)


def dot_bf16(a, b):
    return jnp.dot(a, b, preferred_element_type=jnp.float32)


def column(row):
    eye = lax.broadcasted_iota(jnp.int32, (64, 64), 0) == lax.broadcasted_iota(
        jnp.int32, (64, 64), 1
    )
    col = jnp.sum(jnp.where(eye, row, 0.0), axis=1, keepdims=True)
    return jnp.broadcast_to(col, (64, 256))


def step_kernel(
    state_h, damping_h, mask_h, gain_h, weight_h, pick_h, regrid_h, table_h, own_h, near_h, spec_h,
    fwd_h, inv_h,
    new_state, coef_all, grad_all, half_grad,
    state, damping, mask, gain, weight, pick, regrid, table_x, own, near, spec, fwd, inv,
    q, sec, faces, halo, edge, sink, a, b, gcol, wcol, g_a, g_b, pre, slope,
    fwd_sum, sib_sum, parts, inbox, total, mixed,
    ax, ax_parts,
    load_sem, halo_s, halo_r, sib_s, sib_r, part_s, part_r, mix_s, mix_r, hop_s, hop_r, z_s, z_r,
):
    grp, gx, gy = lax.axis_index("grp"), lax.axis_index("gx"), lax.axis_index("gy")
    chip, core = lax.div(gx, 2), lax.rem(gx, 2)
    cx, cy = lax.div(chip, 4), lax.rem(chip, 4)
    zme = grp * 2 + gy
    sibling = gx + 1 - 2 * core

    along = [[lax.rem(c + step, 4) for step in range(4)] for c in (cx, cy)]

    def chip_at(k, sign):
        return along[0][sign * (k // 4) % 4] * 4 + along[1][sign * (k % 4) % 4]

    def z_at(k):
        zt = lax.rem(zme + k, ZPEERS)
        return {"grp": lax.div(zt, 2), "gy": lax.rem(zt, 2)}

    def hops(k):
        return min(k // 4, 4 - k // 4) + min(k % 4, 4 - k % 4)

    others = sorted(range(1, CHIPS), key=hops)
    far = others[::-1]
    z_far = (4, 3, 5, 2, 6, 1, 7)

    def each(lo, hi, f, unroll=1):
        def step(k, carry):
            f(k)
            return carry
        lax.fori_loop(lo, hi, step, 0, unroll=unroll)

    fwd_parts = [pl.ds(1024 * i, 1024) for i in range(4)]
    moves = [
        (state_h.at[pl.ds(0, 256)], state.at[pl.ds(0, 256)]),
        (regrid_h, regrid),
        (gain_h, gain),
        *((fwd_h.at[part], fwd.at[part]) for part in fwd_parts),
        (state_h.at[pl.ds(256, 744)], state.at[pl.ds(256, 744)]),
        (pick_h, pick),
        (table_h, table_x),
        (damping_h, damping),
        (mask_h, mask),
        (own_h, own),
        (near_h, near),
        (spec_h, spec),
        (weight_h, weight),
        (inv_h, inv.at[:, pl.ds(0, 256)]),
        (inv_h, inv.at[:, pl.ds(256, 256)]),
    ]
    loads = [pltpu.make_async_copy(*m, load_sem.at[i]) for i, m in enumerate(moves)]
    for c in loads[:7]:
        c.start()

    barrier = pltpu.get_barrier_semaphore()

    def greet(target):
        pl.semaphore_signal(barrier, inc=1, device_id=target, device_id_type=MESH)

    for k in others:
        greet({"gx": 2 * chip_at(k, 1) + core})
    greet({"gx": sibling})
    greet({"gx": lax.rem(gx + 2 * core + 31, 32)})
    for k in z_far:
        greet(z_at(k))

    for c in loads[:3]:
        c.wait()
    for c in loads[7:12]:
        c.start()
    q[0:128, 0:128] = state[pl.ds(0, 128, stride=2), :]
    q[0:128, 128:256] = state[pl.ds(1, 128, stride=2), :]
    a[...] = dot_f32(regrid[...], q[0:128, :]).astype(jnp.bfloat16).astype(jnp.float32)
    gcol[...] = column(gain[...])
    fwd_sum[...] = jnp.zeros_like(fwd_sum)
    g_b[...] = jnp.zeros_like(g_b)

    def halo_copy(stage, side):
        to = lax.rem(gx + (1, 31)[side], 32)
        return pltpu.make_async_remote_copy(
            src_ref=faces.at[stage, pl.ds(32 * side, 32)],
            dst_ref=halo.at[stage, side],
            send_sem=halo_s.at[stage, side],
            recv_sem=halo_r.at[stage, side],
            device_id={"gx": to},
            device_id_type=MESH,
        )

    def rows_of(m, r):
        return pl.ds(128 * r + 32 * m, 32)

    def sib_copy(phase, r):
        return pltpu.make_async_remote_copy(
            src_ref=fwd_sum.at[phase, 1 - core, r],
            dst_ref=sib_sum.at[phase, r],
            send_sem=sib_s.at[phase, r],
            recv_sem=sib_r.at[phase, r],
            device_id={"gx": sibling},
            device_id_type=MESH,
        )

    def piece(phase, n):
        first, count = PIECES[phase][n]
        return first, count, pl.ds(first, count)

    def part_copy(phase, n, k):
        rows = piece(phase, n)[2]
        return pltpu.make_async_remote_copy(
            src_ref=parts.at[phase, k, rows],
            dst_ref=inbox.at[phase, k, rows],
            send_sem=part_s.at[phase, n, k],
            recv_sem=part_r.at[phase, n, k],
            device_id={"gx": 2 * chip_at(k, 1) + core},
            device_id_type=MESH,
        )

    def expand(phase, n, k, whose):
        base = chip_at(k, 1) * 128 + 8 * chip + (4 * core if whose == 0 else 4 - 4 * core)
        first, count, unused = piece(phase, n)
        sums = []
        for r in range(first // 32, -(-(first + count) // 32)):
            acc = jnp.zeros((32, 128), jnp.float32)
            for m in range(4):
                rows = pl.ds(32 * m, 32)
                value = (
                    fwd_sum[phase, core, r, rows, :] if whose == 0 else sib_sum[phase, r, rows, :]
                )
                acc = acc + table_x[base + m] * value
            sums.append(acc)
        return sums[0] if len(sums) == 1 else jnp.concatenate(sums, axis=0)

    def prepare(phase, n):
        rows = piece(phase, n)[2]
        for k in (*far, 0):
            parts[phase, k, rows, :] = expand(phase, n, k, 0)

    def scatter(phase, n):
        rows = piece(phase, n)[2]
        for k in far:
            parts[phase, k, rows, :] += expand(phase, n, k, 1)
            part_copy(phase, n, k).start()
        total[phase, rows, :] = parts[phase, 0, rows, :] + expand(phase, n, 0, 1)

    def gather_sum(phase, n):
        rows = piece(phase, n)[2]
        ref = (coef_all, grad_all)[phase]
        summed = total[phase, rows, :]
        for k in others:
            part_copy(phase, n, k).wait_recv()
            summed = summed + inbox[phase, k, rows, :]
        ref[pl.ds(zme, 1), rows, :] = summed[None]

    def z_copy(phase, n, k):
        ref = (coef_all, grad_all)[phase].at[zme, piece(phase, n)[2]]
        return pltpu.make_async_remote_copy(
            src_ref=ref,
            dst_ref=ref,
            send_sem=z_s.at[phase, n, k],
            recv_sem=z_r.at[phase, n, k],
            device_id=z_at(k),
            device_id_type=MESH,
        )

    def transform(phase, i, g, halves):
        points = pl.ds(pl.multiple_of(512 * i, 512), 512)
        both = dot_bf16(g[pl.ds(128 * halves[0], 128 * len(halves)), :], fwd[points, :])
        for n, r in enumerate(halves):
            rows = slice(128 * n, 128 * n + 128)
            fwd_sum[phase, 0, r] += both[rows, 0:128]
            fwd_sum[phase, 1, r] += both[rows, 128:256]

    def lift(j, g, side):
        for m in range(4):
            row = a[pl.ds(m * 16 + j, 1), :]
            for r in range(2):
                x = gcol[pl.ds(32 * r, 32), :] * row
                lifted = x * normal_cdf(x)
                g[rows_of(m, r), 256 * side : 256 * side + 256] = lifted.astype(jnp.bfloat16)

    def lift_four(i):
        part = pl.ds(pl.multiple_of(1024 * i, 1024), 1024)
        pltpu.make_async_copy(fwd_h.at[part], fwd.at[part], load_sem.at[3 + i]).wait()
        lift(4 * i, g_a, 0)
        lift(4 * i + 1, g_a, 1)
        transform(0, jnp.maximum(2 * i - 1, 0), g_b, (0, 1))
        lift(4 * i + 2, g_b, 0)
        lift(4 * i + 3, g_b, 1)
        transform(0, 2 * i, g_a, (0, 1))

    each(0, 4, lift_four)
    transform(0, 7, g_b, (0, 1))
    for c in loads[12:]:
        c.start()

    pl.semaphore_wait(barrier, CHIPS - 1 + 2 + ZPEERS - 1)

    for r in range(2):
        sib_copy(0, r).start()

    lanes = lax.broadcasted_iota(jnp.int32, (32, 256), 1)
    ez = lax.rem(lanes, 16)

    def rates(stage, fields):
        for side in range(2):
            halo_copy(stage, side).wait_recv()
        ends = (gx == 0, gx == 31)
        for side in range(2):
            edge[pl.ds(32 * side, 32), :] = jnp.where(ends[side], 0.0, halo[stage, side])
        low, high = faces[stage, 64:96, :], faces[stage, 96:128, :]
        edge[64:96, :] = jnp.where(lanes < 16, 0.0, pltpu.roll(low, 16, 1))
        edge[96:128, :] = jnp.where(lanes >= 240, 0.0, pltpu.roll(high, 240, 1))
        low, high = faces[stage, 128:160, :], faces[stage, 160:192, :]
        edge[128:160, :] = jnp.where(ez == 0, 0.0, pltpu.roll(low, 1, 1))
        edge[160:192, :] = jnp.where(ez == 15, 0.0, pltpu.roll(high, 255, 1))
        rate = dot_f32(own[...], fields[...]) + dot_f32(near[...], edge[...])
        return rate - sink[...] * fields[...]

    for c in loads[7:12]:
        c.wait()
    q[128:500, 0:128] = state[pl.ds(256, 372, stride=2), :]
    q[128:500, 128:256] = state[pl.ds(257, 372, stride=2), :]
    q[500:512, :] = jnp.zeros((12, 256), jnp.float32)
    sink[...] = mask[...].astype(jnp.float32) * damping[...]
    faces[0, 0:64] = dot_f32(pick[0:64, :], q[...])
    for side in range(2):
        halo_copy(0, side).start()
    prepare(0, 0)
    for r in range(2):
        sib_copy(0, r).wait()
    scatter(0, 0)
    faces[0, 64:192] = dot_f32(pick[64:192, :], q[...])

    for c in loads[12:14]:
        c.wait()
    sec[...] = q[...] + TIME_STEP * rates(0, q)
    faces[1] = dot_f32(pick[...], sec[...])
    for side in range(2):
        halo_copy(1, side).start()

    for n in range(len(PIECES[0])):
        gather_sum(0, n)

    loads[14].wait()

    def mix(i, acc):
        for u in range(8):
            c = i * 8 + u
            row = coef_all[pl.ds(zme, 1), pl.ds(c, 1), :].reshape(1, 128)
            acc = acc + spec[c] * row
        return acc

    mixed[0, 0] = lax.fori_loop(0, 8, mix, jnp.zeros((64, 128), jnp.float32)).astype(jnp.bfloat16)

    def mix_copy(k):
        return pltpu.make_async_remote_copy(
            src_ref=mixed.at[0, 0],
            dst_ref=mixed.at[0, k],
            send_sem=mix_s.at[k],
            recv_sem=mix_r.at[k],
            device_id={"gx": 2 * chip_at(k, 1) + core},
            device_id_type=MESH,
        )

    def hop_copy(k):
        direct = hops(k) > 2
        return pltpu.make_async_remote_copy(
            src_ref=mixed.at[0, 0 if direct else k],
            dst_ref=mixed.at[1, k],
            send_sem=hop_s.at[k],
            recv_sem=hop_r.at[k],
            device_id={"gx": 2 * chip_at(k, 1) + 1 - core if direct else sibling},
            device_id_type=MESH,
        )

    for k in far:
        mix_copy(k).start()
        if hops(k) > 2:
            hop_copy(k).start()
    hop_copy(0).start()
    for n in range(len(PIECES[0])):
        for k in z_far:
            z_copy(0, n, k).start()

    done = 0.5 * (q[...] + sec[...] + TIME_STEP * rates(1, sec))
    new_state[pl.ds(0, 500, stride=2), :] = done[0:500, 0:128]
    new_state[pl.ds(1, 500, stride=2), :] = done[0:500, 128:256]
    b[...] = dot_f32(regrid[...], done[0:128, :]).astype(jnp.bfloat16).astype(jnp.float32)

    def add_modes(half, k, acc):
        base = chip_at(k, -1) * 128 + 4 * gx
        value = mixed[half, k].astype(jnp.float32)
        return tuple(acc[m] + table_x[base + m] * value for m in range(4))

    zeros = tuple(jnp.zeros((64, 128), jnp.float32) for unused in range(4))
    sums = add_modes(0, 0, zeros)
    for k in others:
        mix_copy(k).wait_recv()
        if hops(k) <= 2:
            hop_copy(k).start()
        sums = add_modes(0, k, sums)
    for m in range(4):
        for r in range(2):
            ax[pl.ds(core, 1), rows_of(m, r), :] = sums[m][None, 32 * r : 32 * r + 32]
    sums = zeros
    for k in (0, *others):
        hop_copy(k).wait_recv()
        sums = add_modes(1, k, sums)
    for m in range(4):
        for r in range(2):
            ax[pl.ds(1 - core, 1), rows_of(m, r), :] = sums[m][None, 32 * r : 32 * r + 32]
    for half in range(2):
        value = ax[half]
        high = value.astype(jnp.bfloat16)
        low = (value - high.astype(jnp.float32)).astype(jnp.bfloat16)
        ax_parts[:, 128 * half : 128 * half + 128] = high
        ax_parts[:, 256 + 128 * half : 384 + 128 * half] = low

    loads[15].wait()
    loads[16].wait()
    loads[17].wait()
    wcol[...] = column(weight[...])
    g_b[...] = jnp.zeros_like(g_b)

    def inverse(j, slot):
        pre[slot] = dot_bf16(ax_parts[...], inv[j])

    def back(j, slot, g, side):
        cols = slice(256 * side, 256 * side + 256)
        for m in range(4):
            acc = jnp.zeros((8, 256), jnp.float32)
            for r in range(2):
                rows = rows_of(m, r)
                x = pre[slot, rows, :]
                cdf = normal_cdf(x)
                bell = jnp.exp2(x * x * (-0.5 * LOG2E))
                slope[slot, rows, :] = cdf + x * bell * GAUSS_NORM
                act = x * cdf * wcol[pl.ds(32 * r, 32), :]
                acc = acc + jnp.sum(act.reshape(4, 8, 256), axis=0)
            misfit = jnp.sum(acc, axis=0, keepdims=True) - b[pl.ds(m * 16 + j, 1), :]
            misfit = (2.0 * LOSS_SCALE) * misfit
            for r in range(2):
                rows = rows_of(m, r)
                value = misfit * wcol[pl.ds(32 * r, 32), :] * slope[slot, rows, :]
                g[rows, cols] = value.astype(jnp.bfloat16)

    def back_four(i):
        inverse(4 * i + 1, 1)
        back(4 * i, 0, g_a, 0)
        inverse(4 * i + 2, 0)
        back(4 * i + 1, 1, g_a, 1)
        transform(1, lax.rem(2 * i + 7, 8), g_b, (0, 1))
        inverse(4 * i + 3, 1)
        back(4 * i + 2, 0, g_b, 0)
        inverse(lax.rem(4 * i + 4, 16), 0)
        back(4 * i + 3, 1, g_b, 1)
        transform(1, 2 * i, g_a, (0, 1))

    inverse(0, 0)
    each(0, 4, back_four)
    transform(1, 7, g_b, (0, 1))

    for r in range(2):
        sib_copy(1, r).start()
    for n in range(2):
        prepare(1, n)
    for n in range(2):
        sib_copy(1, n).wait()
        scatter(1, n)
    for n in range(len(PIECES[1])):
        gather_sum(1, n)
        for k in z_far:
            z_copy(1, n, k).start()

    for k in others:
        for phase in range(2):
            for n in range(len(PIECES[phase])):
                part_copy(phase, n, k).wait_send()
        mix_copy(k).wait_send()
    for k in range(CHIPS):
        hop_copy(k).wait_send()
    for stage in range(2):
        for side in range(2):
            halo_copy(stage, side).wait_send()
    for k in z_far:
        z_copy(0, 0, k).wait_recv()
        z_copy(1, 0, k).wait_recv()

    def first_half(c):
        acc = coef_all[0, pl.ds(c, 1), :] * grad_all[0, 0:32, :]
        for t in range(1, ZPEERS):
            acc = acc + coef_all[t, pl.ds(c, 1), :] * grad_all[t, 0:32, :]
        half_grad[pl.ds(c, 1)] = acc[None]

    each(0, 64, first_half, unroll=8)

    for k in z_far:
        z_copy(1, 1, k).wait()
        z_copy(0, 0, k).wait_send()
        z_copy(1, 0, k).wait_send()


def update_kernel(
    coef, grad, half, spec, one, two, state, new_spec, new_one, new_two, new_state,
    out_spec, out_one, out_two, sem,
):
    move = pltpu.make_async_copy(state, new_state, sem.at[0, 3])
    move.start()
    block = 8

    def chunk(i):
        rows = pl.ds(block * i, block)
        return [
            pltpu.make_async_copy(src.at[rows], dst.at[rows], sem.at[i, n])
            for n, (src, dst) in enumerate(
                ((out_spec, new_spec), (out_one, new_one), (out_two, new_two))
            )
        ]

    def run(i, carry):
        for n in range(block):
            c = block * i + n
            acc = coef[0, pl.ds(c, 1), :] * grad[0, 32:64, :]
            for t in range(1, ZPEERS):
                acc = acc + coef[t, pl.ds(c, 1), :] * grad[t, 32:64, :]
            acc = jnp.concatenate([half[c], acc], axis=0)
            m1 = BETA_ONE * one[c].astype(jnp.float32) + (1.0 - BETA_ONE) * acc
            m2 = BETA_TWO * two[c].astype(jnp.float32) + (1.0 - BETA_TWO) * acc * acc
            scaled = m2 * (1.0 / BIAS_TWO)
            den = scaled * lax.rsqrt(scaled) + EPSILON
            inverse = 1.0 / den
            out_spec[c] = spec[c] - (LEARN_RATE / BIAS_ONE) * m1 * inverse
            out_one[c] = m1.astype(jnp.bfloat16)
            out_two[c] = m2.astype(jnp.bfloat16)
        for copy in chunk(i):
            copy.start()
        return carry

    lax.fori_loop(0, 64 // block, run, 0)
    for i in range(64 // block):
        for copy in chunk(i):
            copy.wait()
    move.wait()


def per_device(state, damping, mask, gain, weight, spectral, moment_one, moment_two):
    own, near, pick, regrid, forward, inverse, along_x = tables()
    f32, bf16 = jnp.float32, jnp.bfloat16
    vmem = pl.BlockSpec(memory_space=pltpu.VMEM)
    hbm = pl.BlockSpec(memory_space=pltpu.HBM)
    anywhere = pl.BlockSpec(memory_space=pl.ANY)
    spec_t = jnp.transpose(spectral, (1, 2, 0))
    dma = pltpu.SemaphoreType.DMA
    new_state, coef_all, grad_all, half_grad = pl.pallas_call(
        step_kernel,
        out_shape=(
            jax.ShapeDtypeStruct((1000, 128), f32),
            jax.ShapeDtypeStruct((ZPEERS, 64, 128), f32),
            jax.ShapeDtypeStruct((ZPEERS, 64, 128), f32),
            jax.ShapeDtypeStruct((64, 32, 128), f32),
        ),
        in_specs=[hbm] * 13,
        out_specs=(vmem,) * 4,
        scratch_shapes=[
            pltpu.VMEM((1000, 128), f32),
            pltpu.VMEM((1, 256), f32),
            pltpu.VMEM((1, 256), jnp.int32),
            pltpu.VMEM((1, 64), f32),
            pltpu.VMEM((1, 64), f32),
            pltpu.VMEM((192, 512), f32),
            pltpu.VMEM((64, 128), f32),
            pltpu.SMEM((2048,), f32),
            pltpu.VMEM((512, 512), f32),
            pltpu.VMEM((512, 192), f32),
            pltpu.VMEM((64, 64, 128), f32),
            pltpu.VMEM((4096, 256), bf16),
            pltpu.VMEM((16, 512, 256), bf16),
            pltpu.VMEM((512, 256), f32),
            pltpu.VMEM((512, 256), f32),
            pltpu.VMEM((2, 192, 256), f32),
            pltpu.VMEM((2, 2, 32, 256), f32),
            pltpu.VMEM((192, 256), f32),
            pltpu.VMEM((1, 256), f32),
            pltpu.VMEM((64, 256), f32),
            pltpu.VMEM((64, 256), f32),
            pltpu.VMEM((64, 256), f32),
            pltpu.VMEM((64, 256), f32),
            pltpu.VMEM((256, 512), bf16),
            pltpu.VMEM((256, 512), bf16),
            pltpu.VMEM((2, 256, 256), f32),
            pltpu.VMEM((2, 256, 256), f32),
            pltpu.VMEM((2, 2, 2, 128, 128), f32),
            pltpu.VMEM((2, 2, 128, 128), f32),
            pltpu.VMEM((2, CHIPS, 64, 128), f32),
            pltpu.VMEM((2, CHIPS, 64, 128), f32),
            pltpu.VMEM((2, 64, 128), f32),
            pltpu.VMEM((2, CHIPS, 64, 128), bf16),
            pltpu.VMEM((2, 256, 128), f32),
            pltpu.VMEM((256, 512), bf16),
            dma((18,)),
            dma((2, 2)),
            dma((2, 2)),
            dma((2, 2)),
            dma((2, 2)),
            dma((2, 2, CHIPS)),
            dma((2, 2, CHIPS)),
            dma((CHIPS,)),
            dma((CHIPS,)),
            dma((CHIPS,)),
            dma((CHIPS,)),
            dma((2, 2, ZPEERS)),
            dma((2, 2, ZPEERS)),
        ],
        compiler_params=pltpu.CompilerParams(
            collective_id=0, has_side_effects=True, vmem_limit_bytes=40 * 1024 * 1024
        ),
        name="step",
    )(
        *(
            pltpu.with_memory_space_constraint(v, pltpu.HBM)
            for v in (
                state.reshape(1000, 128), damping, mask, gain.reshape(1, 64), weight.reshape(1, 64),
                pick, regrid, along_x, own, near, spec_t, forward, inverse,
            )
        )
    )
    new_spec, new_one, new_two, new_state = pl.pallas_call(
        update_kernel,
        out_shape=(
            jax.ShapeDtypeStruct((64, 64, 128), f32),
            jax.ShapeDtypeStruct((64, 64, 128), bf16),
            jax.ShapeDtypeStruct((64, 64, 128), bf16),
            jax.ShapeDtypeStruct((1000, 128), f32),
        ),
        in_specs=[vmem] * 6 + [anywhere],
        out_specs=(anywhere,) * 4,
        scratch_shapes=[
            pltpu.VMEM((64, 64, 128), f32),
            pltpu.VMEM((64, 64, 128), bf16),
            pltpu.VMEM((64, 64, 128), bf16),
            dma((8, 4)),
        ],
        compiler_params=pltpu.CompilerParams(vmem_limit_bytes=16 * 1024 * 1024),
        name="update",
    )(
        coef_all, grad_all, half_grad, spec_t,
        jnp.transpose(moment_one, (1, 2, 0)), jnp.transpose(moment_two, (1, 2, 0)), new_state,
    )
    back = (2, 0, 1)
    return (
        new_state.reshape(state.shape),
        jnp.transpose(new_spec, back),
        jnp.transpose(new_one, back),
        jnp.transpose(new_two, back),
    )


def solution(mesh):
    in_specs = (
        P(("grp", "gy"), None, None, "gx", None),
        P("gx", None),
        P("gx", None),
        P(),
        P(),
        P("gx", None, None),
        P("gx", None, None),
        P("gx", None, None),
    )
    out_specs = (
        P(("grp", "gy"), None, None, "gx", None),
        P("gx", None, None),
        P("gx", None, None),
        P("gx", None, None),
    )
    return jax.shard_map(
        per_device, mesh=mesh, in_specs=in_specs, out_specs=out_specs, check_vma=False
    )
```

```python
import math

import jax
import jax.numpy as jnp
import numpy as np
from jax import lax
from jax.experimental import pallas as pl
from jax.experimental.pallas import tpu as pltpu
from jax.sharding import PartitionSpec as P

MESH = pl.DeviceIdType.MESH
HIGHEST = lax.Precision.HIGHEST
KM = 16
CHIPS = 16
ZPEERS = 8
PIECES = (((0, 64),), ((0, 32), (32, 32)))
TIME_STEP = 0.02
FACE_GAIN = 10.0
LOSS_SCALE = 1.0 / 2048.0
LEARN_RATE = 0.001
BETA_ONE = 0.9
BETA_TWO = 0.999
BIAS_ONE = 1.0 - BETA_ONE**10
BIAS_TWO = 1.0 - BETA_TWO**10
EPSILON = 1e-08
HALF_ROOT = 1.0 / math.sqrt(2.0)
GAUSS_NORM = 1.0 / math.sqrt(2.0 * math.pi)
LOG2E = 1.4426950408889634


def lagrange(nodes, column, point):
    value = 1.0
    for other in range(len(nodes)):
        if other != column:
            value = value * (point - nodes[other]) / (nodes[column] - nodes[other])
    return value


def lagrange_slope(nodes, column, point):
    total = 0.0
    for skipped in range(len(nodes)):
        if skipped != column:
            factor = 1.0 / (nodes[column] - nodes[skipped])
            for other in range(len(nodes)):
                if other != column and other != skipped:
                    factor = factor * (point - nodes[other]) / (nodes[column] - nodes[other])
            total = total + factor
    return total


def gll_tables():
    nodes = [-1.0, -math.sqrt(3.0 / 7.0), 0.0, math.sqrt(3.0 / 7.0), 1.0]
    slopes = np.array([[lagrange_slope(nodes, c, nodes[r]) for c in range(5)] for r in range(5)])
    interp = np.array(
        [[lagrange(nodes, c, -1.0 + (2.0 * m + 1.0) / 4.0) for c in range(5)] for m in range(4)]
    )
    return slopes.astype(np.float32), interp.astype(np.float32)


def fourier_table(length, kept):
    angles = np.arange(length) * (2.0 * math.pi / length)
    rows = []
    for freq in range(kept // 2 + 1):
        factor = math.sqrt(1.0 / length) if freq == 0 else math.sqrt(2.0 / length)
        rows.append(factor * np.cos(freq * angles))
    for freq in range(1, kept // 2):
        rows.append(math.sqrt(2.0 / length) * np.sin(freq * angles))
    return np.stack(rows)


def node_of(index, axis, value):
    out = list(index)
    out[axis] = value
    return 25 * out[0] + 5 * out[1] + out[2]


def solver_tables(slopes):
    own = np.zeros((512, 512))
    near = np.zeros((512, 192))
    pick = np.zeros((192, 512))
    for i1 in range(5):
        for i2 in range(5):
            for i3 in range(5):
                index = (i1, i2, i3)
                node = 25 * i1 + 5 * i2 + i3
                for d in range(3):
                    u = 125 * (1 + d)
                    for k in range(5):
                        other = node_of(index, d, k)
                        own[node, u + other] += -2.0 * slopes[index[d], k]
                        own[u + node, other] += -2.0 * slopes[index[d], k]
                    rest = [index[e] for e in range(3) if e != d]
                    face = 5 * rest[0] + rest[1]
                    low, high = 64 * d + face, 64 * d + 32 + face
                    if index[d] == 0:
                        own[node, u + node] -= FACE_GAIN
                        own[node, node] -= FACE_GAIN
                        own[u + node, u + node] -= FACE_GAIN
                        own[u + node, node] -= FACE_GAIN
                        near[node, low] = FACE_GAIN
                        near[u + node, low] = FACE_GAIN
                        pick[high, node] = 1.0
                        pick[high, u + node] = -1.0
                    if index[d] == 4:
                        own[node, u + node] += FACE_GAIN
                        own[node, node] -= FACE_GAIN
                        own[u + node, node] += FACE_GAIN
                        own[u + node, u + node] -= FACE_GAIN
                        near[node, high] = FACE_GAIN
                        near[u + node, high] = -FACE_GAIN
                        pick[low, node] = 1.0
                        pick[low, u + node] = 1.0
    return tuple(t.astype(np.float32) for t in (own, near, pick))


def tables():
    slopes, interp = gll_tables()
    own, near, pick = solver_tables(slopes.astype(np.float64))
    interp = interp.astype(np.float64)
    regrid = np.zeros((64, 128), np.float32)
    regrid[:, :125] = np.kron(np.kron(interp, interp), interp).astype(np.float32)
    joint = np.kron(fourier_table(64, KM), fourier_table(64, KM)).astype(np.float32)
    joint = joint.reshape(256, 16, 4, 16, 4).transpose(2, 4, 0, 1, 3).reshape(16, 256, 256)
    inverse = jnp.asarray(joint).astype(jnp.bfloat16)
    forward = jnp.asarray(joint.transpose(0, 2, 1).reshape(4096, 256)).astype(jnp.bfloat16)
    along_x = jnp.asarray(fourier_table(128, KM), dtype=jnp.float32).astype(jnp.bfloat16)
    along_x = along_x.astype(jnp.float32).reshape(-1)
    return own, near, pick, regrid, forward, inverse, along_x


def normal_cdf(x):
    return 0.5 + 0.5 * lax.erf(x * HALF_ROOT)


def dot_f32(a, b):
    return jnp.dot(a, b, precision=HIGHEST, preferred_element_type=jnp.float32)


def dot_bf16(a, b):
    return jnp.dot(a, b, preferred_element_type=jnp.float32)


def column(row):
    eye = lax.broadcasted_iota(jnp.int32, (64, 64), 0) == lax.broadcasted_iota(
        jnp.int32, (64, 64), 1
    )
    col = jnp.sum(jnp.where(eye, row, 0.0), axis=1, keepdims=True)
    return jnp.broadcast_to(col, (64, 256))


def step_kernel(
    state_h, damping_h, mask_h, gain_h, weight_h, pick_h, regrid_h, table_h, own_h, near_h, spec_h,
    fwd_h, inv_h,
    new_state, coef_all, grad_all, half_grad,
    state, damping, mask, gain, weight, pick, regrid, table_x, own, near, spec, fwd, inv,
    q, sec, faces, halo, edge, sink, a, b, gcol, wcol, g_a, g_b, pre, slope,
    fwd_sum, sib_sum, parts, inbox, total, mixed,
    ax, ax_parts,
    load_sem, halo_s, halo_r, sib_s, sib_r, part_s, part_r, mix_s, mix_r, hop_s, hop_r, z_s, z_r,
):
    grp, gx, gy = lax.axis_index("grp"), lax.axis_index("gx"), lax.axis_index("gy")
    chip, core = lax.div(gx, 2), lax.rem(gx, 2)
    cx, cy = lax.div(chip, 4), lax.rem(chip, 4)
    zme = grp * 2 + gy
    sibling = gx + 1 - 2 * core

    along = [[lax.rem(c + step, 4) for step in range(4)] for c in (cx, cy)]

    def chip_at(k, sign):
        return along[0][sign * (k // 4) % 4] * 4 + along[1][sign * (k % 4) % 4]

    def z_at(k):
        zt = lax.rem(zme + k, ZPEERS)
        return {"grp": lax.div(zt, 2), "gy": lax.rem(zt, 2)}

    def hops(k):
        return min(k // 4, 4 - k // 4) + min(k % 4, 4 - k % 4)

    others = sorted(range(1, CHIPS), key=hops)
    far = others[::-1]
    z_far = (4, 3, 5, 2, 6, 1, 7)

    def each(lo, hi, f, unroll=1):
        def step(k, carry):
            f(k)
            return carry
        lax.fori_loop(lo, hi, step, 0, unroll=unroll)

    fwd_parts = [pl.ds(1024 * i, 1024) for i in range(4)]
    moves = [
        (state_h.at[pl.ds(0, 256)], state.at[pl.ds(0, 256)]),
        (regrid_h, regrid),
        (gain_h, gain),
        *((fwd_h.at[part], fwd.at[part]) for part in fwd_parts),
        (state_h.at[pl.ds(256, 744)], state.at[pl.ds(256, 744)]),
        (pick_h, pick),
        (table_h, table_x),
        (damping_h, damping),
        (mask_h, mask),
        (own_h, own),
        (near_h, near),
        (spec_h, spec),
        (weight_h, weight),
        (inv_h, inv.at[:, pl.ds(0, 256)]),
        (inv_h, inv.at[:, pl.ds(256, 256)]),
    ]
    loads = [pltpu.make_async_copy(*m, load_sem.at[i]) for i, m in enumerate(moves)]
    for c in loads[:7]:
        c.start()

    barrier = pltpu.get_barrier_semaphore()

    def greet(target):
        pl.semaphore_signal(barrier, inc=1, device_id=target, device_id_type=MESH)

    for k in others:
        greet({"gx": 2 * chip_at(k, 1) + core})
    greet({"gx": sibling})
    greet({"gx": lax.rem(gx + 2 * core + 31, 32)})
    for k in z_far:
        greet(z_at(k))

    for c in loads[:3]:
        c.wait()
    for c in loads[7:12]:
        c.start()
    q[0:128, 0:128] = state[pl.ds(0, 128, stride=2), :]
    q[0:128, 128:256] = state[pl.ds(1, 128, stride=2), :]
    a[...] = dot_f32(regrid[...], q[0:128, :]).astype(jnp.bfloat16).astype(jnp.float32)
    gcol[...] = column(gain[...])
    fwd_sum[...] = jnp.zeros_like(fwd_sum)
    g_b[...] = jnp.zeros_like(g_b)

    def halo_copy(stage, side):
        to = lax.rem(gx + (1, 31)[side], 32)
        return pltpu.make_async_remote_copy(
            src_ref=faces.at[stage, pl.ds(32 * side, 32)],
            dst_ref=halo.at[stage, side],
            send_sem=halo_s.at[stage, side],
            recv_sem=halo_r.at[stage, side],
            device_id={"gx": to},
            device_id_type=MESH,
        )

    def rows_of(m, r):
        return pl.ds(128 * r + 32 * m, 32)

    def sib_copy(phase, r):
        return pltpu.make_async_remote_copy(
            src_ref=fwd_sum.at[phase, 1 - core, r],
            dst_ref=sib_sum.at[phase, r],
            send_sem=sib_s.at[phase, r],
            recv_sem=sib_r.at[phase, r],
            device_id={"gx": sibling},
            device_id_type=MESH,
        )

    def piece(phase, n):
        first, count = PIECES[phase][n]
        return first, count, pl.ds(first, count)

    def part_copy(phase, n, k):
        rows = piece(phase, n)[2]
        return pltpu.make_async_remote_copy(
            src_ref=parts.at[phase, k, rows],
            dst_ref=inbox.at[phase, k, rows],
            send_sem=part_s.at[phase, n, k],
            recv_sem=part_r.at[phase, n, k],
            device_id={"gx": 2 * chip_at(k, 1) + core},
            device_id_type=MESH,
        )

    def expand(phase, n, k, whose):
        base = chip_at(k, 1) * 128 + 8 * chip + (4 * core if whose == 0 else 4 - 4 * core)
        first, count, unused = piece(phase, n)
        sums = []
        for r in range(first // 32, -(-(first + count) // 32)):
            acc = jnp.zeros((32, 128), jnp.float32)
            for m in range(4):
                rows = pl.ds(32 * m, 32)
                value = (
                    fwd_sum[phase, core, r, rows, :] if whose == 0 else sib_sum[phase, r, rows, :]
                )
                acc = acc + table_x[base + m] * value
            sums.append(acc)
        return sums[0] if len(sums) == 1 else jnp.concatenate(sums, axis=0)

    def prepare(phase, n):
        rows = piece(phase, n)[2]
        for k in (*far, 0):
            parts[phase, k, rows, :] = expand(phase, n, k, 0)

    def scatter(phase, n):
        rows = piece(phase, n)[2]
        for k in far:
            parts[phase, k, rows, :] += expand(phase, n, k, 1)
            part_copy(phase, n, k).start()
        total[phase, rows, :] = parts[phase, 0, rows, :] + expand(phase, n, 0, 1)

    def gather_sum(phase, n):
        rows = piece(phase, n)[2]
        ref = (coef_all, grad_all)[phase]
        summed = total[phase, rows, :]
        for k in others:
            part_copy(phase, n, k).wait_recv()
            summed = summed + inbox[phase, k, rows, :]
        ref[pl.ds(zme, 1), rows, :] = summed[None]

    def z_copy(phase, n, k):
        ref = (coef_all, grad_all)[phase].at[zme, piece(phase, n)[2]]
        return pltpu.make_async_remote_copy(
            src_ref=ref,
            dst_ref=ref,
            send_sem=z_s.at[phase, n, k],
            recv_sem=z_r.at[phase, n, k],
            device_id=z_at(k),
            device_id_type=MESH,
        )

    def transform(phase, i, g, halves):
        points = pl.ds(pl.multiple_of(512 * i, 512), 512)
        both = dot_bf16(g[pl.ds(128 * halves[0], 128 * len(halves)), :], fwd[points, :])
        for n, r in enumerate(halves):
            rows = slice(128 * n, 128 * n + 128)
            fwd_sum[phase, 0, r] += both[rows, 0:128]
            fwd_sum[phase, 1, r] += both[rows, 128:256]

    def lift(j, g, side):
        for m in range(4):
            row = a[pl.ds(m * 16 + j, 1), :]
            for r in range(2):
                x = gcol[pl.ds(32 * r, 32), :] * row
                lifted = x * normal_cdf(x)
                g[rows_of(m, r), 256 * side : 256 * side + 256] = lifted.astype(jnp.bfloat16)

    def lift_four(i):
        part = pl.ds(pl.multiple_of(1024 * i, 1024), 1024)
        pltpu.make_async_copy(fwd_h.at[part], fwd.at[part], load_sem.at[3 + i]).wait()
        lift(4 * i, g_a, 0)
        lift(4 * i + 1, g_a, 1)
        transform(0, jnp.maximum(2 * i - 1, 0), g_b, (0, 1))
        lift(4 * i + 2, g_b, 0)
        lift(4 * i + 3, g_b, 1)
        transform(0, 2 * i, g_a, (0, 1))

    each(0, 4, lift_four)
    transform(0, 7, g_b, (0, 1))
    for c in loads[12:]:
        c.start()

    pl.semaphore_wait(barrier, CHIPS - 1 + 2 + ZPEERS - 1)

    for r in range(2):
        sib_copy(0, r).start()

    lanes = lax.broadcasted_iota(jnp.int32, (32, 256), 1)
    ez = lax.rem(lanes, 16)

    def rates(stage, fields):
        for side in range(2):
            halo_copy(stage, side).wait_recv()
        ends = (gx == 0, gx == 31)
        for side in range(2):
            edge[pl.ds(32 * side, 32), :] = jnp.where(ends[side], 0.0, halo[stage, side])
        low, high = faces[stage, 64:96, :], faces[stage, 96:128, :]
        edge[64:96, :] = jnp.where(lanes < 16, 0.0, pltpu.roll(low, 16, 1))
        edge[96:128, :] = jnp.where(lanes >= 240, 0.0, pltpu.roll(high, 240, 1))
        low, high = faces[stage, 128:160, :], faces[stage, 160:192, :]
        edge[128:160, :] = jnp.where(ez == 0, 0.0, pltpu.roll(low, 1, 1))
        edge[160:192, :] = jnp.where(ez == 15, 0.0, pltpu.roll(high, 255, 1))
        rate = dot_f32(own[...], fields[...]) + dot_f32(near[...], edge[...])
        return rate - sink[...] * fields[...]

    for c in loads[7:12]:
        c.wait()
    q[128:500, 0:128] = state[pl.ds(256, 372, stride=2), :]
    q[128:500, 128:256] = state[pl.ds(257, 372, stride=2), :]
    q[500:512, :] = jnp.zeros((12, 256), jnp.float32)
    sink[...] = mask[...].astype(jnp.float32) * damping[...]
    faces[0, 0:64] = dot_f32(pick[0:64, :], q[...])
    for side in range(2):
        halo_copy(0, side).start()
    prepare(0, 0)
    for r in range(2):
        sib_copy(0, r).wait()
    scatter(0, 0)
    faces[0, 64:192] = dot_f32(pick[64:192, :], q[...])

    for c in loads[12:14]:
        c.wait()
    sec[...] = q[...] + TIME_STEP * rates(0, q)
    faces[1] = dot_f32(pick[...], sec[...])
    for side in range(2):
        halo_copy(1, side).start()

    for n in range(len(PIECES[0])):
        gather_sum(0, n)

    loads[14].wait()

    def mix(i, acc):
        for u in range(8):
            c = i * 8 + u
            row = coef_all[pl.ds(zme, 1), pl.ds(c, 1), :].reshape(1, 128)
            acc = acc + spec[c] * row
        return acc

    mixed[0, 0] = lax.fori_loop(0, 8, mix, jnp.zeros((64, 128), jnp.float32)).astype(jnp.bfloat16)

    def mix_copy(k):
        return pltpu.make_async_remote_copy(
            src_ref=mixed.at[0, 0],
            dst_ref=mixed.at[0, k],
            send_sem=mix_s.at[k],
            recv_sem=mix_r.at[k],
            device_id={"gx": 2 * chip_at(k, 1) + core},
            device_id_type=MESH,
        )

    def hop_copy(k):
        direct = hops(k) > 3
        return pltpu.make_async_remote_copy(
            src_ref=mixed.at[0, 0 if direct else k],
            dst_ref=mixed.at[1, k],
            send_sem=hop_s.at[k],
            recv_sem=hop_r.at[k],
            device_id={"gx": 2 * chip_at(k, 1) + 1 - core if direct else sibling},
            device_id_type=MESH,
        )

    for k in far:
        mix_copy(k).start()
        if hops(k) > 3:
            hop_copy(k).start()
    hop_copy(0).start()
    for n in range(len(PIECES[0])):
        for k in z_far:
            z_copy(0, n, k).start()

    done = 0.5 * (q[...] + sec[...] + TIME_STEP * rates(1, sec))
    new_state[pl.ds(0, 500, stride=2), :] = done[0:500, 0:128]
    new_state[pl.ds(1, 500, stride=2), :] = done[0:500, 128:256]
    b[...] = dot_f32(regrid[...], done[0:128, :]).astype(jnp.bfloat16).astype(jnp.float32)

    def add_modes(half, k, acc):
        base = chip_at(k, -1) * 128 + 4 * gx
        value = mixed[half, k].astype(jnp.float32)
        return tuple(acc[m] + table_x[base + m] * value for m in range(4))

    zeros = tuple(jnp.zeros((64, 128), jnp.float32) for unused in range(4))
    sums = add_modes(0, 0, zeros)
    for k in others:
        mix_copy(k).wait_recv()
        if hops(k) <= 3:
            hop_copy(k).start()
        sums = add_modes(0, k, sums)
    for m in range(4):
        for r in range(2):
            ax[pl.ds(core, 1), rows_of(m, r), :] = sums[m][None, 32 * r : 32 * r + 32]
    sums = zeros
    for k in (0, *others):
        hop_copy(k).wait_recv()
        sums = add_modes(1, k, sums)
    for m in range(4):
        for r in range(2):
            ax[pl.ds(1 - core, 1), rows_of(m, r), :] = sums[m][None, 32 * r : 32 * r + 32]
    for half in range(2):
        value = ax[half]
        high = value.astype(jnp.bfloat16)
        low = (value - high.astype(jnp.float32)).astype(jnp.bfloat16)
        ax_parts[:, 128 * half : 128 * half + 128] = high
        ax_parts[:, 256 + 128 * half : 384 + 128 * half] = low

    loads[15].wait()
    loads[16].wait()
    loads[17].wait()
    wcol[...] = column(weight[...])
    g_b[...] = jnp.zeros_like(g_b)

    def inverse(j, slot):
        pre[slot] = dot_bf16(ax_parts[...], inv[j])

    def back(j, slot, g, side):
        cols = slice(256 * side, 256 * side + 256)
        for m in range(4):
            acc = jnp.zeros((8, 256), jnp.float32)
            for r in range(2):
                rows = rows_of(m, r)
                x = pre[slot, rows, :]
                cdf = normal_cdf(x)
                bell = jnp.exp2(x * x * (-0.5 * LOG2E))
                slope[slot, rows, :] = cdf + x * bell * GAUSS_NORM
                act = x * cdf * wcol[pl.ds(32 * r, 32), :]
                acc = acc + jnp.sum(act.reshape(4, 8, 256), axis=0)
            misfit = jnp.sum(acc, axis=0, keepdims=True) - b[pl.ds(m * 16 + j, 1), :]
            misfit = (2.0 * LOSS_SCALE) * misfit
            for r in range(2):
                rows = rows_of(m, r)
                value = misfit * wcol[pl.ds(32 * r, 32), :] * slope[slot, rows, :]
                g[rows, cols] = value.astype(jnp.bfloat16)

    def back_four(i):
        inverse(4 * i + 1, 1)
        back(4 * i, 0, g_a, 0)
        inverse(4 * i + 2, 0)
        back(4 * i + 1, 1, g_a, 1)
        transform(1, lax.rem(2 * i + 7, 8), g_b, (0, 1))
        inverse(4 * i + 3, 1)
        back(4 * i + 2, 0, g_b, 0)
        inverse(lax.rem(4 * i + 4, 16), 0)
        back(4 * i + 3, 1, g_b, 1)
        transform(1, 2 * i, g_a, (0, 1))

    inverse(0, 0)
    each(0, 4, back_four)
    transform(1, 7, g_b, (0, 1))

    for r in range(2):
        sib_copy(1, r).start()
    for n in range(2):
        prepare(1, n)
    for n in range(2):
        sib_copy(1, n).wait()
        scatter(1, n)
    for n in range(len(PIECES[1])):
        gather_sum(1, n)
        for k in z_far:
            z_copy(1, n, k).start()

    for k in others:
        for phase in range(2):
            for n in range(len(PIECES[phase])):
                part_copy(phase, n, k).wait_send()
        mix_copy(k).wait_send()
    for k in range(CHIPS):
        hop_copy(k).wait_send()
    for stage in range(2):
        for side in range(2):
            halo_copy(stage, side).wait_send()
    for k in z_far:
        z_copy(0, 0, k).wait_recv()
        z_copy(1, 0, k).wait_recv()

    def first_half(c):
        acc = coef_all[0, pl.ds(c, 1), :] * grad_all[0, 0:32, :]
        for t in range(1, ZPEERS):
            acc = acc + coef_all[t, pl.ds(c, 1), :] * grad_all[t, 0:32, :]
        half_grad[pl.ds(c, 1)] = acc[None]

    each(0, 64, first_half, unroll=8)

    for k in z_far:
        z_copy(1, 1, k).wait()
        z_copy(0, 0, k).wait_send()
        z_copy(1, 0, k).wait_send()


def update_kernel(
    coef, grad, half, spec, one, two, state, new_spec, new_one, new_two, new_state,
    out_spec, out_one, out_two, sem,
):
    move = pltpu.make_async_copy(state, new_state, sem.at[0, 3])
    move.start()
    block = 8

    def chunk(i):
        rows = pl.ds(block * i, block)
        return [
            pltpu.make_async_copy(src.at[rows], dst.at[rows], sem.at[i, n])
            for n, (src, dst) in enumerate(
                ((out_spec, new_spec), (out_one, new_one), (out_two, new_two))
            )
        ]

    def run(i, carry):
        for n in range(block):
            c = block * i + n
            acc = coef[0, pl.ds(c, 1), :] * grad[0, 32:64, :]
            for t in range(1, ZPEERS):
                acc = acc + coef[t, pl.ds(c, 1), :] * grad[t, 32:64, :]
            acc = jnp.concatenate([half[c], acc], axis=0)
            m1 = BETA_ONE * one[c].astype(jnp.float32) + (1.0 - BETA_ONE) * acc
            m2 = BETA_TWO * two[c].astype(jnp.float32) + (1.0 - BETA_TWO) * acc * acc
            scaled = m2 * (1.0 / BIAS_TWO)
            den = scaled * lax.rsqrt(scaled) + EPSILON
            inverse = 1.0 / den
            out_spec[c] = spec[c] - (LEARN_RATE / BIAS_ONE) * m1 * inverse
            out_one[c] = m1.astype(jnp.bfloat16)
            out_two[c] = m2.astype(jnp.bfloat16)
        for copy in chunk(i):
            copy.start()
        return carry

    lax.fori_loop(0, 64 // block, run, 0)
    for i in range(64 // block):
        for copy in chunk(i):
            copy.wait()
    move.wait()


def per_device(state, damping, mask, gain, weight, spectral, moment_one, moment_two):
    own, near, pick, regrid, forward, inverse, along_x = tables()
    f32, bf16 = jnp.float32, jnp.bfloat16
    vmem = pl.BlockSpec(memory_space=pltpu.VMEM)
    hbm = pl.BlockSpec(memory_space=pltpu.HBM)
    anywhere = pl.BlockSpec(memory_space=pl.ANY)
    spec_t = jnp.transpose(spectral, (1, 2, 0))
    dma = pltpu.SemaphoreType.DMA
    new_state, coef_all, grad_all, half_grad = pl.pallas_call(
        step_kernel,
        out_shape=(
            jax.ShapeDtypeStruct((1000, 128), f32),
            jax.ShapeDtypeStruct((ZPEERS, 64, 128), f32),
            jax.ShapeDtypeStruct((ZPEERS, 64, 128), f32),
            jax.ShapeDtypeStruct((64, 32, 128), f32),
        ),
        in_specs=[hbm] * 13,
        out_specs=(vmem,) * 4,
        scratch_shapes=[
            pltpu.VMEM((1000, 128), f32),
            pltpu.VMEM((1, 256), f32),
            pltpu.VMEM((1, 256), jnp.int32),
            pltpu.VMEM((1, 64), f32),
            pltpu.VMEM((1, 64), f32),
            pltpu.VMEM((192, 512), f32),
            pltpu.VMEM((64, 128), f32),
            pltpu.SMEM((2048,), f32),
            pltpu.VMEM((512, 512), f32),
            pltpu.VMEM((512, 192), f32),
            pltpu.VMEM((64, 64, 128), f32),
            pltpu.VMEM((4096, 256), bf16),
            pltpu.VMEM((16, 512, 256), bf16),
            pltpu.VMEM((512, 256), f32),
            pltpu.VMEM((512, 256), f32),
            pltpu.VMEM((2, 192, 256), f32),
            pltpu.VMEM((2, 2, 32, 256), f32),
            pltpu.VMEM((192, 256), f32),
            pltpu.VMEM((1, 256), f32),
            pltpu.VMEM((64, 256), f32),
            pltpu.VMEM((64, 256), f32),
            pltpu.VMEM((64, 256), f32),
            pltpu.VMEM((64, 256), f32),
            pltpu.VMEM((256, 512), bf16),
            pltpu.VMEM((256, 512), bf16),
            pltpu.VMEM((2, 256, 256), f32),
            pltpu.VMEM((2, 256, 256), f32),
            pltpu.VMEM((2, 2, 2, 128, 128), f32),
            pltpu.VMEM((2, 2, 128, 128), f32),
            pltpu.VMEM((2, CHIPS, 64, 128), f32),
            pltpu.VMEM((2, CHIPS, 64, 128), f32),
            pltpu.VMEM((2, 64, 128), f32),
            pltpu.VMEM((2, CHIPS, 64, 128), bf16),
            pltpu.VMEM((2, 256, 128), f32),
            pltpu.VMEM((256, 512), bf16),
            dma((18,)),
            dma((2, 2)),
            dma((2, 2)),
            dma((2, 2)),
            dma((2, 2)),
            dma((2, 2, CHIPS)),
            dma((2, 2, CHIPS)),
            dma((CHIPS,)),
            dma((CHIPS,)),
            dma((CHIPS,)),
            dma((CHIPS,)),
            dma((2, 2, ZPEERS)),
            dma((2, 2, ZPEERS)),
        ],
        compiler_params=pltpu.CompilerParams(
            collective_id=0, has_side_effects=True, vmem_limit_bytes=40 * 1024 * 1024
        ),
        name="step",
    )(
        *(
            pltpu.with_memory_space_constraint(v, pltpu.HBM)
            for v in (
                state.reshape(1000, 128), damping, mask, gain.reshape(1, 64), weight.reshape(1, 64),
                pick, regrid, along_x, own, near, spec_t, forward, inverse,
            )
        )
    )
    new_spec, new_one, new_two, new_state = pl.pallas_call(
        update_kernel,
        out_shape=(
            jax.ShapeDtypeStruct((64, 64, 128), f32),
            jax.ShapeDtypeStruct((64, 64, 128), bf16),
            jax.ShapeDtypeStruct((64, 64, 128), bf16),
            jax.ShapeDtypeStruct((1000, 128), f32),
        ),
        in_specs=[vmem] * 6 + [anywhere],
        out_specs=(anywhere,) * 4,
        scratch_shapes=[
            pltpu.VMEM((64, 64, 128), f32),
            pltpu.VMEM((64, 64, 128), bf16),
            pltpu.VMEM((64, 64, 128), bf16),
            dma((8, 4)),
        ],
        compiler_params=pltpu.CompilerParams(vmem_limit_bytes=16 * 1024 * 1024),
        name="update",
    )(
        coef_all, grad_all, half_grad, spec_t,
        jnp.transpose(moment_one, (1, 2, 0)), jnp.transpose(moment_two, (1, 2, 0)), new_state,
    )
    back = (2, 0, 1)
    return (
        new_state.reshape(state.shape),
        jnp.transpose(new_spec, back),
        jnp.transpose(new_one, back),
        jnp.transpose(new_two, back),
    )


def solution(mesh):
    in_specs = (
        P(("grp", "gy"), None, None, "gx", None),
        P("gx", None),
        P("gx", None),
        P(),
        P(),
        P("gx", None, None),
        P("gx", None, None),
        P("gx", None, None),
    )
    out_specs = (
        P(("grp", "gy"), None, None, "gx", None),
        P("gx", None, None),
        P("gx", None, None),
        P("gx", None, None),
    )
    return jax.shard_map(
        per_device, mesh=mesh, in_specs=in_specs, out_specs=out_specs, check_vma=False
    )
```
